32 devices in a mesh: gx: 4 (over z), gz: 8 (over y, x, core).
Axes of the slice: x: 2, y: 2, z: 4, core: 2. Of those that a mesh axis runs over, the one named last changes fastest.
Arguments:
- velocity: float32 [256, 64, 256], P('gx', 'gz'), may hold values from -6 to 6
- viscosity: float32 [256, 64, 256], P('gx', 'gz'), may hold values from 0.5 to 5
- force: float32 [256, 64, 256], P('gx', 'gz'), may hold values from -30 to 30
Outputs:
- increment: float32 [256, 64, 256], P('gx', 'gz')
The draws below stay inside these ranges and needn't reach their ends.
All inputs are finite; a program needn't handle non-finite values.
Results may differ from the reference program's by a relative error of at most 0.0005.
Values sent between devices are 32-bit elements; how exact they have to be, the bound alone decides.
No kernel may reach another device: no remote copies, remote signals or barrier semaphores. Data moves between devices by JAX's collectives and lax.ppermute only.
A program may use at most 128 MiB of HBM per device.

```python
import math
import jax
import jax.numpy as jnp
from jax import lax

NY = 256
NX = 256
NZ = 64


def draw_force(key, part):
    noise_part = jax.random.normal(key, (NX, NZ, NY), jnp.float32)
    return jnp.clip(6.0 * noise_part, -30.0, 30.0)


def shard_levels(stream_key, extent, shards, low, top_value):
    level = 1.0
    for dim, shards_of in shards:
        steps = jax.random.uniform(jax.random.fold_in(jax.random.fold_in(stream_key, 6), dim), (shards_of,), jnp.float32, low / len(shards), top_value / len(shards))
        level = level * jnp.repeat(jnp.exp(steps), extent[dim] // shards_of).reshape((-1,) + (1,) * (len(extent) - 1 - dim))
    return level


def centred(key, shape, width, most, cuts=(), kind=jnp.bfloat16):
    array = width * jax.random.normal(key, shape, jnp.float32)
    if cuts:
        array = array * shard_levels(key, shape, cuts, -0.22, 0.18)
    return jnp.clip(array, -most, most).astype(kind)


def setup_inputs(seed: int = 0) -> dict:
    arg_keys = jax.random.split(jax.random.key(seed), 4)
    return {
        "velocity": centred(arg_keys[0], (NX, NZ, NY), 1.0, 6.0, ((0, 4), (1, 8)), jnp.float32),
        "viscosity": jnp.clip(jnp.exp(math.log(5.0) - 2.3025851 * jax.random.uniform(arg_keys[1], (NX, NZ, NY), jnp.float32) ** shard_levels(arg_keys[1], (NX, NZ, NY), ((0, 4), (1, 8)), -0.2, 0.2)), 0.5, 5.0),
        "force": draw_force(jax.random.fold_in(arg_keys[3], 71), 0),
    }


IMPLICIT_WEIGHT = 0.5
SCALE_ALONG_X = 1600.0
SCALE_ALONG_Y = 0.5
SCALE_ALONG_Z = 400.0


def beside(values, which_dim):
    length = values.shape[which_dim]
    widths = [(1, 1) if k == which_dim else (0, 0) for k in range(values.ndim)]
    padded = jnp.pad(values, widths)
    return (lax.slice_in_dim(padded, 0, length, axis=which_dim),
            lax.slice_in_dim(padded, 2, length + 2, axis=which_dim))


def face_terms(viscosity, which_dim, factor):
    before, beyond = beside(viscosity, which_dim)
    return factor * 0.5 * (viscosity + before), factor * 0.5 * (viscosity + beyond)


def apply_part(field, k_low, k_high, which_dim):
    before, beyond = beside(field, which_dim)
    return k_high * (beyond - field) - k_low * (field - before)


def thomas(k_low, k_high, source, which_dim):
    lower_band = -IMPLICIT_WEIGHT * k_low
    upper_band = -IMPLICIT_WEIGHT * k_high
    middle = 1.0 + IMPLICIT_WEIGHT * (k_low + k_high)
    stacked = tuple(jnp.moveaxis(t, which_dim, 0) for t in (lower_band, middle, upper_band, source))
    zero_row = jnp.zeros(stacked[0].shape[1:], jnp.float32)

    def forward(carried, entries):
        c_prev, d_prev = carried
        a, b, c, d = entries
        pivots = b - a * c_prev
        c_next = c / pivots
        d_next = (d - a * d_prev) / pivots
        return (c_next, d_next), (c_next, d_next)

    unused, (c_all, d_all) = lax.scan(forward, (zero_row, zero_row), stacked)

    def backward(next_value, entries):
        c, d = entries
        result = d - c * next_value
        return result, result

    unused, solved = lax.scan(backward, zero_row, (c_all, d_all), reverse=True)
    return jnp.moveaxis(solved, 0, which_dim)


def reference(velocity, viscosity, force):
    explicit = force
    for which_dim, factor in ((0, SCALE_ALONG_X), (1, SCALE_ALONG_Z), (2, SCALE_ALONG_Y)):
        k_low, k_high = face_terms(viscosity, which_dim, factor)
        explicit = explicit + apply_part(velocity, k_low, k_high, which_dim)
    k_low, k_high = face_terms(viscosity, 0, SCALE_ALONG_X)
    first = thomas(k_low, k_high, explicit, 0)
    k_low, k_high = face_terms(viscosity, 2, SCALE_ALONG_Y)
    second = thomas(k_low, k_high, first, 2)
    k_low, k_high = face_terms(viscosity, 1, SCALE_ALONG_Z)
    return thomas(k_low, k_high, second, 1)
```

```python
import jax
import jax.numpy as jnp
from jax import lax
from jax.experimental import pallas as pl
from jax.experimental.pallas import tpu as pltpu
from jax.sharding import PartitionSpec as P

HALF_X = 0.5 * 1600.0 * 0.5
HALF_Y = 0.5 * 0.5 * 0.5
HALF_Z = 0.5 * 400.0 * 0.5

F32 = jnp.float32
VMEM = pl.BlockSpec(memory_space=pltpu.VMEM)
SMEM = pl.BlockSpec(memory_space=pltpu.SMEM)


def call(kernel, outs, n_in, scratch=(), cost=None):
    return pl.pallas_call(
        kernel,
        out_shape=tuple(jax.ShapeDtypeStruct(s, F32) for s in outs),
        in_specs=[SMEM] + [VMEM] * (n_in - 1),
        out_specs=tuple(VMEM for _ in outs),
        scratch_shapes=list(scratch),
        compiler_params=pltpu.CompilerParams(vmem_limit_bytes=48 << 20),
        cost_estimate=cost,
    )


def cost(elements, ops, touched):
    return pl.CostEstimate(flops=elements * ops, bytes_accessed=touched * 4, transcendentals=0)


def iota(shape, dim):
    return lax.broadcasted_iota(jnp.int32, shape, dim)


def shift(x, s, axis):
    return pltpu.roll(x, s % x.shape[axis], axis)


def x_factor_kernel(pos, visc, vel, force, c_out, n_out, gf_out, gl_out, coef, rhs, cf, cb):
    rows, depth, width = visc.shape
    mid = rows // 2
    lo_wall = jnp.where(pos[0] == 0, HALF_X, 0.0)
    hi_wall = jnp.where(pos[0] == pos[1] - 1, HALF_X, 0.0)
    s = 1.0 + lo_wall * visc[0]
    t = 1.0 + hi_wall * visc[rows - 1]
    lo_term = s - 1.0
    hi_term = t - 1.0
    for i in range(rows - 1):
        e = HALF_X * (visc[i] + visc[i + 1])
        r = 1.0 / (s + e)
        c = e * r
        cf[i] = c
        if i < mid:
            c_out[i] = c
            n_out[i] = r
        s = 1.0 + c * s
        if i + 1 == mid:
            s_mid = s
        j = rows - 1 - i
        e = HALF_X * (visc[j] + visc[j - 1])
        r = 1.0 / (t + e)
        c = e * r
        cb[j] = c
        if j > mid:
            c_out[j] = c
            n_out[j] = r
        t = 1.0 + c * t
        if j - 1 == mid:
            t_mid = t
    n_out[mid] = 1.0 / (s_mid + t_mid - 1.0)
    c_out[mid] = jnp.zeros_like(s)
    gl = 1.0 / (s + hi_term)
    gf = 1.0 / (t + lo_term)
    coef[0] = gf
    coef[2] = gl
    coef[3] = visc[0]
    coef[4] = visc[rows - 1]
    gl_out[rows - 1] = gl
    gf_out[0] = gf
    for i in range(rows - 1):
        gl = cf[rows - 2 - i] * gl
        gl_out[rows - 2 - i] = gl
        gf = cb[i + 1] * gf
        gf_out[i + 1] = gf
    coef[1] = gl

    lane = iota((depth, width), 1)
    sub = iota((depth, width), 0)
    for i in range(rows):
        v = vel[i]
        nu = visc[i]
        vn = jnp.where(lane == width - 1, 0.0, shift(v, -1, 1))
        nn = jnp.where(lane == width - 1, 0.0, shift(nu, -1, 1))
        fy = (2.0 * HALF_Y) * (nu + nn) * (vn - v)
        fl = jnp.where(lane == 0, (2.0 * HALF_Y) * nu * v, shift(fy, 1, 1))
        fz = (2.0 * HALF_Z) * (nu + shift(nu, -1, 0)) * (shift(v, -1, 0) - v)
        fz = jnp.where(sub == depth - 1, 0.0, fz)
        rhs[i] = force[i] + 2.0 * v + (fy - fl) + (fz - shift(fz, 1, 0))


def z_factor_kernel(pos, visc, al, ga, inv, gf_out, gl_out, planes):
    rows, depth, width = visc.shape
    lo_wall = jnp.where(pos[2] == 0, HALF_Z, 0.0)
    hi_wall = jnp.where(pos[2] == pos[3] - 1, HALF_Z, 0.0)
    sub = iota((depth, width), 0)
    wall = jnp.where(sub == 0, lo_wall, jnp.where(sub == depth - 1, hi_wall, 0.0))
    first = jnp.where(sub == 0, 1.0, 0.0)
    last = jnp.where(sub == depth - 1, 1.0, 0.0)
    for i in range(rows):
        nu = visc[i]
        e = jnp.where(sub == depth - 1, 0.0, HALF_Z * (nu + shift(nu, -1, 0)))
        sigma = 1.0 + wall * nu
        b = sigma + e + shift(e, 1, 0)
        gf, gl = first, last
        s, k = 1, 0
        while s < depth:
            r = 1.0 / b
            a = shift(e * r, s, 0)
            g = e * shift(r, -s, 0)
            al[k, i] = a
            ga[k, i] = g
            e = g * shift(e, -s, 0)
            sigma = sigma + a * shift(sigma, s, 0) + g * shift(sigma, -s, 0)
            gf = gf + a * shift(gf, s, 0) + g * shift(gf, -s, 0)
            gl = gl + a * shift(gl, s, 0) + g * shift(gl, -s, 0)
            s *= 2
            k += 1
            b = sigma + e + shift(e, s, 0) if s < depth else sigma
        r = 1.0 / b
        gf = gf * r
        gl = gl * r
        inv[i] = r
        gf_out[i] = gf
        gl_out[i] = gl
        planes[0, i] = gf[0]
        planes[1, i] = gf[depth - 1]
        planes[2, i] = gl[depth - 1]


def y_factor_kernel(pos, visc, al, ga, inv):
    rows, depth, width = visc.shape
    block = 4
    shape = (block, depth, width)
    lane = iota(shape, 2)

    def body(i, carry):
        at = pl.ds(i * block, block)
        nu = visc[at]
        wall = jnp.where((lane == 0) | (lane == width - 1), HALF_Y, 0.0) * nu
        e = jnp.where(lane == width - 1, 0.0, HALF_Y * (nu + shift(nu, -1, 2)))
        b = 1.0 + wall + e + shift(e, 1, 2)
        s, k = 1, 0
        while s < width:
            r = 1.0 / b
            er = e * r
            a = shift(er, s, 2)
            g = e * shift(r, -s, 2)
            al[k, at] = a
            ga[k, at] = g
            b = b - g * e - shift(er * e, s, 2)
            e = g * shift(e, -s, 2)
            s *= 2
            k += 1
        inv[at] = 1.0 / b
        return carry

    lax.fori_loop(0, rows // block, body, 0)


def x_solve_kernel(pos, visc, vel, rhs0, c_in, n_in, coef, pair, cross, w_out, payload):
    rows, depth, width = visc.shape
    mid = rows // 2
    sub = iota((depth, width), 0)
    upper = lax.rem(pos[2], 2)
    from_pair = (sub >= depth // 2) == (upper == 0)
    edge = (sub == 0) | (sub == depth - 1)

    def rhs(i):
        n_vel = jnp.where(from_pair, pair[0, pl.ds(i, 1)], cross[0, pl.ds(i, 1)])
        n_visc = jnp.where(from_pair, pair[1, pl.ds(i, 1)], cross[1, pl.ds(i, 1)])
        extra = (2.0 * HALF_Z) * (visc[i] + n_visc) * (n_vel - vel[i])
        return rhs0[i] + jnp.where(edge, extra, 0.0)

    d = rhs(0)
    w_out[0] = d
    u = rhs(rows - 1)
    w_out[rows - 1] = u
    for i in range(1, mid):
        d = rhs(i) + c_in[i - 1] * d
        w_out[i] = d
        j = rows - 1 - i
        if j > mid:
            u = rhs(j) + c_in[j + 1] * u
            w_out[j] = u
    d = rhs(mid) + c_in[mid - 1] * d + c_in[mid + 1] * u
    d = d * n_in[mid]
    w_out[mid] = d
    u = d
    for i in range(1, mid + 1):
        j = mid - i
        d = w_out[j] * n_in[j] + c_in[j] * d
        w_out[j] = d
        j = mid + i
        if j < rows:
            u = w_out[j] * n_in[j] + c_in[j] * u
            w_out[j] = u
    payload[0] = d
    payload[1] = u
    for k in range(5):
        payload[2 + k] = coef[k]


def make_middle_kernel(n):
    def kernel(pos, *refs):
        parts = refs[:n]
        (w, gf, gl, vel, yal, yga, yinv, zal, zga, zinv, dz, ends, slots, flux) = refs[n:]
        rows, depth, width = w.shape
        me = pos[0]
        for k in range(n):
            slots[jnp.bitwise_xor(me, k)] = parts[k][...]
        zero = jnp.zeros((depth, width), F32)
        flux[0] = zero
        flux[n] = zero
        lower, source = [], []
        for f in range(n - 1):
            e = HALF_X * (slots[f, 6] + slots[f + 1, 5])
            pivot = 1.0 / e + slots[f, 4] + slots[f + 1, 2]
            right = slots[f + 1, 0] - slots[f, 1]
            if f:
                pivot = pivot - slots[f, 3] * lower[-1]
                right = right + lower[-1] * source[-1]
            r = 1.0 / pivot
            lower.append(slots[f + 1, 3] * r)
            source.append(right)
            flux[f + 1] = right * r
        q = flux[n - 1] if n > 1 else zero
        for f in reversed(range(n - 2)):
            q = flux[f + 1] + lower[f] * q
            flux[f + 1] = q
        q_left = flux[me]
        q_right = flux[me + 1]
        block = 4
        steps_y = yal.shape[0]
        steps_z = zal.shape[0]

        def body(i, carry):
            at = pl.ds(i * block, block)
            d = w[at] + q_right * gl[at] - q_left * gf[at] - 2.0 * vel[at]
            for k in range(steps_y):
                d = d + yal[k, at] * shift(d, 1 << k, 2) + yga[k, at] * shift(d, -(1 << k), 2)
            d = d * yinv[at]
            for k in range(steps_z):
                d = d + zal[k, at] * shift(d, 1 << k, 1) + zga[k, at] * shift(d, -(1 << k), 1)
            d = d * zinv[at]
            dz[at] = d
            for j in range(block):
                ends[0, pl.ds(i * block + j, 1)] = d[j, 0:1]
                ends[1, pl.ds(i * block + j, 1)] = d[j, depth - 1:depth]
            return carry

        lax.fori_loop(0, rows // block, body, 0)

    return kernel


def final_kernel(pos, dz, gf, gl, q_left, q_right, out):
    rows = dz.shape[0]
    for i in range(rows):
        out[i] = dz[i] + q_right[pl.ds(i, 1)] * gl[i] - q_left[pl.ds(i, 1)] * gf[i]


def ordered(parts, me):
    bit = 1
    parts = list(parts)
    while bit < len(parts):
        odd = (me & bit) != 0
        parts = [jnp.where(odd, parts[i ^ bit], parts[i]) for i in range(len(parts))]
        bit *= 2
    return parts


def local(velocity, viscosity, force):
    rows, depth, width = velocity.shape
    nx, nz = lax.axis_size("gx"), lax.axis_size("gz")
    chips = nz // 2
    ix, iz = lax.axis_index("gx"), lax.axis_index("gz")
    upper = iz % 2
    chip = iz // 2
    pos = jnp.stack([ix, jnp.int32(nx), iz, jnp.int32(nz)]).astype(jnp.int32)
    volume = (rows, depth, width)
    size = rows * depth * width
    steps_y = (width - 1).bit_length()
    steps_z = (depth - 1).bit_length()

    pair_route = [(i, i ^ 1) for i in range(nz)]
    cross_route = [(i, i + 1 if i % 2 else i - 1) for i in range(1, nz - 1)]
    both = jnp.stack([velocity, viscosity])
    near_z = jnp.where(upper == 0, depth - 1, 0)
    far_z = jnp.where(upper == 0, 0, depth - 1)
    to_pair = lax.dynamic_index_in_dim(both, near_z, 2, keepdims=False)
    to_cross = lax.dynamic_index_in_dim(both, far_z, 2, keepdims=False)
    pair = lax.ppermute(to_pair, "gz", pair_route)
    cross = lax.ppermute(to_cross, "gz", cross_route)

    plane = (depth, width)
    slab = (rows, width)
    c_x, n_x, gf_x, gl_x, coef, rhs0 = call(
        x_factor_kernel,
        [volume] * 4 + [(5,) + plane, volume], 4,
        [pltpu.VMEM(volume, F32)] * 2, cost(size, 60, 9 * size),
    )(pos, viscosity, velocity, force)
    al_z, ga_z, inv_z, gf_z, gl_z, planes = call(
        z_factor_kernel,
        [(steps_z,) + volume] * 2 + [volume] * 3 + [(3,) + slab], 2, (), cost(size, 60, 10 * size),
    )(pos, viscosity)
    al_y, ga_y, inv_y = call(
        y_factor_kernel, [(steps_y,) + volume] * 2 + [volume], 2, (), cost(size, 200, 18 * size)
    )(pos, viscosity)

    w, payload = call(
        x_solve_kernel, [volume, (7,) + plane], 9, (), cost(size, 20, 6 * size)
    )(pos, viscosity, velocity, rhs0, c_x, n_x, coef, pair, cross)
    parts = [payload] + [
        lax.ppermute(payload, "gx", [(i, i ^ k) for i in range(nx)]) for k in range(1, nx)
    ]

    right_face = jnp.where(upper == 0, pair[1], cross[1])
    reach = 1.0 / (HALF_Z * (viscosity[:, depth - 1] + right_face))
    own_c = jnp.concatenate([planes, reach[None]])
    mate_c = lax.ppermute(own_c, "gz", pair_route)
    low_c = jnp.where(upper == 0, own_c, mate_c)
    high_c = jnp.where(upper == 0, mate_c, own_c)
    weight = 1.0 / (low_c[3] + low_c[2] + high_c[0])
    low_fl, high_fl = low_c[1], high_c[1]
    chip_c = jnp.stack([
        low_c[0] - weight * low_fl * low_fl,
        weight * low_fl * high_fl,
        high_c[2] - weight * high_fl * high_fl + high_c[3],
    ])
    groups = [[2 * c + p for c in range(chips)] for p in range(2)]
    all_c = lax.all_gather(chip_c, "gz", axis_index_groups=groups)

    dz, ends = call(
        make_middle_kernel(nx), [volume, (2,) + slab], 11 + nx,
        [pltpu.VMEM((nx, 7) + plane, F32), pltpu.VMEM((nx + 1,) + plane, F32)],
        cost(size, 100, 32 * size),
    )(pos, *parts, w, gf_x, gl_x, velocity, al_y, ga_y, inv_y, al_z, ga_z, inv_z)

    mate = lax.ppermute(ends, "gz", pair_route)
    low = jnp.where(upper == 0, ends, mate)
    high = jnp.where(upper == 0, mate, ends)
    jump = high[0] - low[1]
    q_mid = weight * jump
    chip_ends = jnp.stack([low[0] + low_fl * q_mid, high[1] - high_fl * q_mid])
    others = [chip_ends] + [
        lax.ppermute(chip_ends, "gz", [(i, i ^ (2 * k)) for i in range(nz)])
        for k in range(1, chips)
    ]
    by_chip = ordered(others, chip)
    lower, source, fluxes = [], [], []
    for f in range(chips - 1):
        pivot = all_c[f, 2] + all_c[f + 1, 0]
        right = by_chip[f + 1][0] - by_chip[f][1]
        if f:
            pivot = pivot - all_c[f, 1] * lower[-1]
            right = right + lower[-1] * source[-1]
        r = 1.0 / pivot
        lower.append(all_c[f + 1, 1] * r)
        source.append(right)
        fluxes.append(right * r)
    for f in reversed(range(chips - 2)):
        fluxes[f] = fluxes[f] + lower[f] * fluxes[f + 1]
    zero = jnp.zeros(slab, F32)
    chip_left, chip_right = zero, zero
    for f in range(chips - 1):
        chip_right = jnp.where(chip == f, fluxes[f], chip_right)
        chip_left = jnp.where(chip == f + 1, fluxes[f], chip_left)
    q_mid = weight * (jump + chip_right * high_fl + chip_left * low_fl)
    q_left = jnp.where(upper == 0, chip_left, q_mid)
    q_right = jnp.where(upper == 0, q_mid, chip_right)
    return call(final_kernel, [volume], 6, (), cost(size, 4, 4 * size))(
        pos, dz, gf_z, gl_z, q_left, q_right
    )[0]


def solution(mesh):
    return jax.shard_map(
        local,
        mesh=mesh,
        in_specs=(P("gx", "gz", None), P("gx", "gz", None), P("gx", "gz", None)),
        out_specs=P("gx", "gz", None),
        check_vma=False,
    )
```

```python
import jax
import jax.numpy as jnp
from jax import lax
from jax.experimental import pallas as pl
from jax.experimental.pallas import tpu as pltpu
from jax.sharding import PartitionSpec as P

HALF_X = 0.5 * 1600.0 * 0.5
HALF_Y = 0.5 * 0.5 * 0.5
HALF_Z = 0.5 * 400.0 * 0.5
Y_CHUNKS = 8

F32 = jnp.float32
VMEM = pl.BlockSpec(memory_space=pltpu.VMEM)
SMEM = pl.BlockSpec(memory_space=pltpu.SMEM)
HBM = pl.BlockSpec(memory_space=pltpu.HBM)


def call(kernel, outs, ins, scratch=(), flops=0, touched=0, out_specs=None):
    return pl.pallas_call(
        kernel,
        out_shape=tuple(jax.ShapeDtypeStruct(s, F32) for s in outs),
        in_specs=[SMEM] + ins,
        out_specs=tuple(out_specs or [VMEM] * len(outs)),
        scratch_shapes=list(scratch),
        compiler_params=pltpu.CompilerParams(vmem_limit_bytes=8 << 20),
        cost_estimate=pl.CostEstimate(
            flops=flops, bytes_accessed=4 * touched, transcendentals=0
        ),
    )


def iota(shape, dim):
    return lax.broadcasted_iota(jnp.int32, shape, dim)


def shift(x, s, axis):
    return pltpu.roll(x, s % x.shape[axis], axis)


def factor(
    nu, rows, half, lo_term, hi_term, c_out, n_out, gf_out, gl_out, cf, cb,
    beside_pivots=lambda i: None, beside_responses=lambda i: None,
):
    mid = rows // 2
    s, t = 1.0 + lo_term, 1.0 + hi_term
    for i in range(rows - 1):
        e = half * (nu(i) + nu(i + 1))
        r = 1.0 / (s + e)
        c = e * r
        cf[i] = c
        if i < mid:
            c_out[i] = c
            n_out[i] = r
        s = 1.0 + c * s
        if i + 1 == mid:
            s_mid = s
        j = rows - 1 - i
        e = half * (nu(j) + nu(j - 1))
        r = 1.0 / (t + e)
        c = e * r
        cb[j] = c
        if j > mid:
            c_out[j] = c
            n_out[j] = r
        t = 1.0 + c * t
        if j - 1 == mid:
            t_mid = t
        beside_pivots(i)
    n_out[mid] = 1.0 / (s_mid + t_mid - 1.0)
    gl = 1.0 / (s + hi_term)
    gf = 1.0 / (t + lo_term)
    beside_pivots(rows - 1)
    ends = [gf, None, gl]
    gl_out[rows - 1] = gl
    gf_out[0] = gf
    for i in range(rows - 1):
        gl = cf[rows - 2 - i] * gl
        gl_out[rows - 2 - i] = gl
        gf = cb[i + 1] * gf
        gf_out[i + 1] = gf
        beside_responses(i)
    beside_responses(rows - 1)
    ends[1] = gl
    return ends


def block_solve(rhs, rows, c, n, out):
    mid = rows // 2
    d = rhs(0)
    out[0] = d
    u = rhs(rows - 1)
    out[rows - 1] = u
    for i in range(1, mid):
        d = rhs(i) + c[i - 1] * d
        out[i] = d
        j = rows - 1 - i
        if j > mid:
            u = rhs(j) + c[j + 1] * u
            out[j] = u
    d = (rhs(mid) + c[mid - 1] * d + c[mid + 1] * u) * n[mid]
    out[mid] = d
    u = d
    for i in range(1, mid + 1):
        j = mid - i
        d = out[j] * n[j] + c[j] * d
        out[j] = d
        j = mid + i
        if j < rows:
            u = out[j] * n[j] + c[j] * u
            out[j] = u
    return d, u


def load_kernel(pos, visc_hbm, vel_hbm, visc, vel, visc_z, near, far, vel_z, sems):
    rows, depth, width = visc.shape
    copies = []
    half = rows // 2
    for k, (src, dst) in enumerate(((visc_hbm, visc), (vel_hbm, vel))):
        for p in range(2):
            at = pl.ds(p * half, half)
            copies.append(pltpu.make_async_copy(src.at[at], dst.at[at], sems.at[k, p]))
    for c in copies:
        c.start()
    upper = lax.rem(pos[2], 2)
    near_at = (1 - upper) * (depth - 1)
    far_at = upper * (depth - 1)
    for k, (dst, turned) in enumerate(((visc, visc_z), (vel, vel_z))):
        for p in range(2):
            copies[2 * k + p].wait()
        turned[...] = jnp.transpose(dst[...], (1, 0, 2))
        near[1 - k] = turned[near_at]
        far[1 - k] = turned[far_at]


def x_factor_kernel(pos, visc, vel, force_hbm, c, n, gf, gl, coef, rhs, cf, cb, force, sem):
    rows, depth, width = visc.shape
    copy = pltpu.make_async_copy(force_hbm, force, sem)
    copy.start()
    lo_wall = jnp.where(pos[0] == 0, HALF_X, 0.0)
    hi_wall = jnp.where(pos[0] == pos[1] - 1, HALF_X, 0.0)
    lane = iota((depth, width), 1)
    sub = iota((depth, width), 0)

    def explicit(i):
        v = vel[i]
        nu = visc[i]
        vn = jnp.where(lane == width - 1, 0.0, shift(v, -1, 1))
        nn = jnp.where(lane == width - 1, 0.0, shift(nu, -1, 1))
        fy = (2.0 * HALF_Y) * (nu + nn) * (vn - v)
        fl = jnp.where(lane == 0, (2.0 * HALF_Y) * nu * v, shift(fy, 1, 1))
        fz = (2.0 * HALF_Z) * (nu + shift(nu, -1, 0)) * (shift(v, -1, 0) - v)
        fz = jnp.where(sub == depth - 1, 0.0, fz)
        rhs[i] = 2.0 * v + (fy - fl) + (fz - shift(fz, 1, 0))

    def add_force(i):
        if i == 0:
            copy.wait()
        rhs[i] = rhs[i] + force[i]

    ends = factor(
        lambda i: visc[i], rows, HALF_X, lo_wall * visc[0], hi_wall * visc[rows - 1],
        c, n, gf, gl, cf, cb, explicit, add_force,
    )
    for k in range(3):
        coef[k] = ends[k]
    coef[3] = visc[0]
    coef[4] = visc[rows - 1]


def z_factor_kernel(pos, visc_z, c, n, gf, gl, planes, cf, cb):
    depth = visc_z.shape[0]
    lo_wall = jnp.where(pos[2] == 0, HALF_Z, 0.0)
    hi_wall = jnp.where(pos[2] == pos[3] - 1, HALF_Z, 0.0)
    ends = factor(
        lambda i: visc_z[i], depth, HALF_Z, lo_wall * visc_z[0], hi_wall * visc_z[depth - 1],
        c, n, gf, gl, cf, cb,
    )
    for k in range(3):
        planes[k] = ends[k]


def to_lines(block):
    lines, width = block.shape
    turned = block.T.reshape(Y_CHUNKS, width // Y_CHUNKS, lines)
    return jnp.transpose(turned, (1, 0, 2))


def from_lines(block):
    length, chunks, lines = block.shape
    return jnp.transpose(block, (1, 0, 2)).reshape(length * chunks, lines).T


def y_factor_kernel(pos, visc, c, n, gf, gl, al, ga, inv, nu, cf, cb):
    rows, depth, width = visc.shape
    length, chunks, lines = c.shape
    group = 128 // depth
    for g in range(rows // group):
        block = visc[g * group:(g + 1) * group].reshape(128, width)
        nu[:, :, g * 128:(g + 1) * 128] = to_lines(block)
    sub = iota((chunks, lines), 0)
    lo = jnp.where(sub == 0, HALF_Y * nu[0], 0.0)
    hi = jnp.where(sub == chunks - 1, HALF_Y * nu[length - 1], 0.0)
    first, across, last = factor(
        lambda i: nu[i], length, HALF_Y, lo, hi, c, n, gf, gl, cf, cb
    )
    inner = sub < chunks - 1
    e = HALF_Y * (nu[length - 1] + shift(nu[0], -1, 0))
    b = jnp.where(inner, 1.0 / e + last + shift(first, -1, 0), 1.0)
    o = jnp.where(sub < chunks - 2, shift(across, -1, 0), 0.0)
    s, k = 1, 0
    while s < chunks:
        r = 1.0 / b
        a = shift(o * r, s, 0)
        g = o * shift(r, -s, 0)
        al[k] = a
        ga[k] = g
        b = b - g * o - a * shift(o, s, 0)
        o = g * shift(o, -s, 0)
        s *= 2
        k += 1
    inv[...] = 1.0 / b


def x_solve_kernel(pos, visc, vel, rhs0, c, n, coef, near, far, pair, cross, w, payload, edge_lo, edge_hi):
    rows, depth, width = visc.shape
    sub = iota((depth, width), 0)
    upper = lax.rem(pos[2], 2)
    two = 2.0 * HALF_Z
    by_pair = two * (near[1] + pair[1]) * (pair[0] - near[0])
    by_cross = two * (far[1] + cross[1]) * (cross[0] - far[0])
    edge_lo[...] = jnp.where(upper == 0, by_cross, by_pair)
    edge_hi[...] = jnp.where(upper == 0, by_pair, by_cross)

    def rhs(i):
        at = pl.ds(i, 1)
        lo = jnp.where(sub == 0, edge_lo[at], 0.0)
        return rhs0[i] + jnp.where(sub == depth - 1, edge_hi[at], lo)

    d, u = block_solve(rhs, rows, c, n, w)
    payload[0] = d
    payload[1] = u
    for k in range(5):
        payload[2 + k] = coef[k]


def make_middle_kernel(parts_n):
    def kernel(pos, *refs):
        parts = refs[:parts_n]
        (w, gf, gl, vel, cy, ny, gfy, gly, aly, gay, invy, cz, nz,
         dz, ends, slots, flux, src, sol, turned) = refs[parts_n:]
        rows, depth, width = w.shape
        me = pos[0]
        for k in range(parts_n):
            slots[jnp.bitwise_xor(me, k)] = parts[k][...]
        zero = jnp.zeros((depth, width), F32)
        flux[0] = zero
        flux[parts_n] = zero
        lower, source = [], []
        for f in range(parts_n - 1):
            e = HALF_X * (slots[f, 6] + slots[f + 1, 5])
            pivot = 1.0 / e + slots[f, 4] + slots[f + 1, 2]
            right = slots[f + 1, 0] - slots[f, 1]
            if f:
                pivot = pivot - slots[f, 3] * lower[-1]
                right = right + lower[-1] * source[-1]
            r = 1.0 / pivot
            lower.append(slots[f + 1, 3] * r)
            source.append(right)
            flux[f + 1] = right * r
        q = flux[parts_n - 1]
        for f in reversed(range(parts_n - 2)):
            q = flux[f + 1] + lower[f] * q
            flux[f + 1] = q
        q_left = flux[me]
        q_right = flux[me + 1]

        group = 128 // depth
        for g in range(rows // group):
            at = pl.ds(g * group, group)
            d = w[at] + q_right * gl[at] - q_left * gf[at] - 2.0 * vel[at]
            src[:, :, g * 128:(g + 1) * 128] = to_lines(d.reshape(128, width))

        length, chunks, lines = src.shape
        sub = iota((chunks, lines), 0)
        d, u = block_solve(lambda i: src[i], length, cy, ny, sol)
        q = jnp.where(sub < chunks - 1, shift(d, -1, 0) - u, 0.0)
        for k in range(aly.shape[0]):
            q = q + aly[k] * shift(q, 1 << k, 0) + gay[k] * shift(q, -(1 << k), 0)
        q = q * invy[...]
        ql = shift(q, 1, 0)
        for i in range(length):
            sol[i] = sol[i] + q * gly[i] - ql * gfy[i]
        for g in range(rows // group):
            block = from_lines(sol[:, :, g * 128:(g + 1) * 128])
            block = block.reshape(group, depth, width)
            turned[:, g * group:(g + 1) * group, :] = jnp.transpose(block, (1, 0, 2))
        d, u = block_solve(lambda i: turned[i], depth, cz, nz, dz)
        ends[0] = d
        ends[1] = u

    return kernel


def final_kernel(pos, dz, gf, gl, q_left, q_right, out, buf, sems):
    depth, rows, width = dz.shape
    parts = buf.shape[0]
    group = rows // parts
    copies = []
    for p in range(parts):
        at = slice(p * group, (p + 1) * group)
        d = dz[:, at] + q_right[at] * gl[:, at] - q_left[at] * gf[:, at]
        buf[p] = jnp.transpose(d, (1, 0, 2))
        copy = pltpu.make_async_copy(buf.at[p], out.at[pl.ds(p * group, group)], sems.at[p])
        copy.start()
        copies.append(copy)
    for copy in copies:
        copy.wait()


def ordered(parts, me):
    bit = 1
    parts = list(parts)
    while bit < len(parts):
        odd = (me & bit) != 0
        parts = [jnp.where(odd, parts[i ^ bit], parts[i]) for i in range(len(parts))]
        bit *= 2
    return parts


def local(velocity, viscosity, force):
    rows, depth, width = velocity.shape
    nx, nz = lax.axis_size("gx"), lax.axis_size("gz")
    chips = nz // 2
    ix, iz = lax.axis_index("gx"), lax.axis_index("gz")
    upper = iz % 2
    chip = iz // 2
    pos = jnp.stack([ix, jnp.int32(nx), iz, jnp.int32(nz)]).astype(jnp.int32)
    volume = (rows, depth, width)
    zmajor = (depth, rows, width)
    lines = (width // Y_CHUNKS, Y_CHUNKS, rows * depth)
    size = rows * depth * width
    plane = (depth, width)
    slab = (rows, width)
    y_steps = (Y_CHUNKS - 1).bit_length()

    pair_route = [(i, i ^ 1) for i in range(nz)]
    cross_route = [(i, i + 1 if i % 2 else i - 1) for i in range(1, nz - 1)]

    def to_chip(k):
        return [(i, i ^ (2 * k)) for i in range(nz)]

    visc, vel, visc_z, near, far = call(
        load_kernel, [volume, volume, zmajor, (2,) + slab, (2,) + slab], [HBM, HBM],
        [pltpu.VMEM(zmajor, F32), pltpu.SemaphoreType.DMA((2, 2))], size, 6 * size,
    )(pos, viscosity, velocity)
    pair = lax.ppermute(near, "gz", pair_route)
    cross = lax.ppermute(far, "gz", cross_route)

    c_z, n_z, gf_z, gl_z, planes = call(
        z_factor_kernel, [zmajor] * 4 + [(3,) + slab], [VMEM],
        [pltpu.VMEM(zmajor, F32)] * 2, 20 * size, 5 * size,
    )(pos, visc_z)
    c_x, n_x, gf_x, gl_x, coef, rhs0 = call(
        x_factor_kernel, [volume] * 4 + [(5,) + plane, volume], [VMEM, VMEM, HBM],
        [pltpu.VMEM(volume, F32)] * 3 + [pltpu.SemaphoreType.DMA(())], 60 * size, 9 * size,
    )(pos, visc, vel, force)
    c_y, n_y, gf_y, gl_y, al_y, ga_y, inv_y = call(
        y_factor_kernel, [lines] * 4 + [(y_steps,) + lines[1:]] * 2 + [lines[1:]], [VMEM],
        [pltpu.VMEM(lines, F32)] * 3, 30 * size, 6 * size,
    )(pos, visc)

    mate_c = lax.ppermute(planes, "gz", pair_route)

    w, payload = call(
        x_solve_kernel, [volume, (7,) + plane], [VMEM] * 10,
        [pltpu.VMEM(slab, F32)] * 2, 20 * size, 6 * size,
    )(pos, visc, vel, rhs0, c_x, n_x, coef, near, far, pair, cross)
    mid_reach = 1.0 / (HALF_Z * (near[1] + pair[1]))
    end_reach = 1.0 / (HALF_Z * (far[1] + cross[1]))
    low_c = jnp.where(upper == 0, planes, mate_c)
    high_c = jnp.where(upper == 0, mate_c, planes)
    weight = 1.0 / (mid_reach + low_c[2] + high_c[0])
    low_fl, high_fl = low_c[1], high_c[1]
    chip_c = jnp.stack([
        low_c[0] - weight * low_fl * low_fl + jnp.where(upper == 0, end_reach, 0.0),
        weight * low_fl * high_fl,
        high_c[2] - weight * high_fl * high_fl + jnp.where(upper == 0, 0.0, end_reach),
    ])
    payload, chip_c = lax.optimization_barrier((payload, chip_c))
    parts = [payload] + [
        lax.ppermute(payload, "gx", [(i, i ^ k) for i in range(nx)]) for k in range(1, nx)
    ]
    all_c = ordered(
        [chip_c] + [lax.ppermute(chip_c, "gz", to_chip(k)) for k in range(1, chips)], chip
    )
    lower, inverse = [], []
    for f in range(chips - 1):
        pivot = all_c[f][2] + all_c[f + 1][0]
        if f:
            pivot = pivot - all_c[f][1] * lower[-1]
        inverse.append(1.0 / pivot)
        lower.append(all_c[f + 1][1] * inverse[-1])

    dz, ends = call(
        make_middle_kernel(nx), [zmajor, (2,) + slab], [VMEM] * (nx + 13),
        [pltpu.VMEM((nx, 7) + plane, F32), pltpu.VMEM((nx + 1,) + plane, F32),
         pltpu.VMEM(lines, F32), pltpu.VMEM(lines, F32), pltpu.VMEM(zmajor, F32)],
        60 * size, 14 * size,
    )(pos, *parts, w, gf_x, gl_x, vel, c_y, n_y, gf_y, gl_y, al_y, ga_y, inv_y, c_z, n_z)

    mate = lax.ppermute(ends, "gz", pair_route)
    low = jnp.where(upper == 0, ends, mate)
    high = jnp.where(upper == 0, mate, ends)
    jump = high[0] - low[1]
    q_mid = weight * jump
    chip_ends = jnp.stack([low[0] + low_fl * q_mid, high[1] - high_fl * q_mid])
    by_chip = ordered(
        [chip_ends] + [lax.ppermute(chip_ends, "gz", to_chip(k)) for k in range(1, chips)], chip
    )
    source, fluxes = [], []
    for f in range(chips - 1):
        right = by_chip[f + 1][0] - by_chip[f][1]
        if f:
            right = right + lower[f - 1] * source[-1]
        source.append(right)
        fluxes.append(right * inverse[f])
    for f in reversed(range(chips - 2)):
        fluxes[f] = fluxes[f] + lower[f] * fluxes[f + 1]
    chip_left = chip_right = jnp.zeros(slab, F32)
    for f in range(chips - 1):
        chip_right = jnp.where(chip == f, fluxes[f], chip_right)
        chip_left = jnp.where(chip == f + 1, fluxes[f], chip_left)
    q_mid = weight * (jump + chip_right * high_fl + chip_left * low_fl)
    q_left = jnp.where(upper == 0, chip_left, q_mid)
    q_right = jnp.where(upper == 0, q_mid, chip_right)
    return call(
        final_kernel, [volume], [VMEM] * 5,
        [pltpu.VMEM((4, rows // 4, depth, width), F32), pltpu.SemaphoreType.DMA((4,))],
        4 * size, 4 * size, [HBM],
    )(pos, dz, gf_z, gl_z, q_left, q_right)[0]


def solution(mesh):
    return jax.shard_map(
        local,
        mesh=mesh,
        in_specs=(P("gx", "gz", None), P("gx", "gz", None), P("gx", "gz", None)),
        out_specs=P("gx", "gz", None),
        check_vma=False,
    )
```

```python
import jax
import jax.numpy as jnp
from jax import lax
from jax.experimental import pallas as pl
from jax.experimental.pallas import tpu as pltpu
from jax.sharding import PartitionSpec as P

HALF_X = 0.5 * 1600.0 * 0.5
HALF_Y = 0.5 * 0.5 * 0.5
HALF_Z = 0.5 * 400.0 * 0.5
Y_CHUNKS = 8

F32 = jnp.float32
VMEM = pl.BlockSpec(memory_space=pltpu.VMEM)
HBM = pl.BlockSpec(memory_space=pltpu.HBM)


def call(kernel, outs, ins, scratch=(), flops=0, touched=0, out_specs=None):
    return pl.pallas_call(
        kernel,
        out_shape=tuple(jax.ShapeDtypeStruct(s, F32) for s in outs),
        in_specs=ins,
        out_specs=tuple(out_specs or [VMEM] * len(outs)),
        scratch_shapes=list(scratch),
        compiler_params=pltpu.CompilerParams(vmem_limit_bytes=8 << 20),
        cost_estimate=pl.CostEstimate(
            flops=flops, bytes_accessed=4 * touched, transcendentals=0
        ),
    )


def iota(shape, dim):
    return lax.broadcasted_iota(jnp.int32, shape, dim)


def shift(x, s, axis):
    return pltpu.roll(x, s % x.shape[axis], axis)


def factor(
    nu, rows, half, lo_term, hi_term, c_out, n_out, gf_out, gl_out, cf, cb,
    beside_pivots=lambda i: None, beside_responses=lambda i: None,
):
    mid = rows // 2
    s, t = 1.0 + lo_term, 1.0 + hi_term
    for i in range(rows - 1):
        e = half * (nu(i) + nu(i + 1))
        r = 1.0 / (s + e)
        c = e * r
        cf[i] = c
        if i < mid:
            c_out[i] = c
            n_out[i] = r
        s = 1.0 + c * s
        if i + 1 == mid:
            s_mid = s
        j = rows - 1 - i
        e = half * (nu(j) + nu(j - 1))
        r = 1.0 / (t + e)
        c = e * r
        cb[j] = c
        if j > mid:
            c_out[j] = c
            n_out[j] = r
        t = 1.0 + c * t
        if j - 1 == mid:
            t_mid = t
        beside_pivots(i)
    n_out[mid] = 1.0 / (s_mid + t_mid - 1.0)
    gl = 1.0 / (s + hi_term)
    gf = 1.0 / (t + lo_term)
    beside_pivots(rows - 1)
    ends = [gf, None, gl]
    gl_out[rows - 1] = gl
    gf_out[0] = gf
    for i in range(rows - 1):
        gl = cf[rows - 2 - i] * gl
        gl_out[rows - 2 - i] = gl
        gf = cb[i + 1] * gf
        gf_out[i + 1] = gf
        beside_responses(i)
    beside_responses(rows - 1)
    ends[1] = gl
    return ends


def block_solve(rhs, rows, c, n, out):
    mid = rows // 2
    d = rhs(0)
    out[0] = d
    u = rhs(rows - 1)
    out[rows - 1] = u
    for i in range(1, mid):
        d = rhs(i) + c[i - 1] * d
        out[i] = d
        j = rows - 1 - i
        if j > mid:
            u = rhs(j) + c[j + 1] * u
            out[j] = u
    d = (rhs(mid) + c[mid - 1] * d + c[mid + 1] * u) * n[mid]
    out[mid] = d
    u = d
    for i in range(1, mid + 1):
        j = mid - i
        d = out[j] * n[j] + c[j] * d
        out[j] = d
        j = mid + i
        if j < rows:
            u = out[j] * n[j] + c[j] * u
            out[j] = u
    return d, u


def turn_kernel(visc, vel, visc_z, near, far, vel_z):
    depth = visc.shape[1]
    upper = lax.rem(lax.axis_index("gz"), 2)
    near_at = (1 - upper) * (depth - 1)
    far_at = upper * (depth - 1)
    for k, (src, turned) in enumerate(((vel, vel_z), (visc, visc_z))):
        turned[...] = jnp.transpose(src[...], (1, 0, 2))
        near[k] = turned[near_at]
        far[k] = turned[far_at]


def x_factor_kernel(visc, vel, force_hbm, c, n, gf, gl, coef, rhs, cf, cb, force, sem):
    rows, depth, width = visc.shape
    copy = pltpu.make_async_copy(force_hbm, force, sem)
    copy.start()
    lo_wall = jnp.where(lax.axis_index("gx") == 0, HALF_X, 0.0)
    hi_wall = jnp.where(lax.axis_index("gx") == lax.axis_size("gx") - 1, HALF_X, 0.0)
    lane = iota((depth, width), 1)
    sub = iota((depth, width), 0)

    def explicit(i):
        v = vel[i]
        nu = visc[i]
        vn = jnp.where(lane == width - 1, 0.0, shift(v, -1, 1))
        nn = jnp.where(lane == width - 1, 0.0, shift(nu, -1, 1))
        fy = (2.0 * HALF_Y) * (nu + nn) * (vn - v)
        fl = jnp.where(lane == 0, (2.0 * HALF_Y) * nu * v, shift(fy, 1, 1))
        fz = (2.0 * HALF_Z) * (nu + shift(nu, -1, 0)) * (shift(v, -1, 0) - v)
        fz = jnp.where(sub == depth - 1, 0.0, fz)
        rhs[i] = 2.0 * v + (fy - fl) + (fz - shift(fz, 1, 0))

    def add_force(i):
        if i == 0:
            copy.wait()
        rhs[i] = rhs[i] + force[i]

    ends = factor(
        lambda i: visc[i], rows, HALF_X, lo_wall * visc[0], hi_wall * visc[rows - 1],
        c, n, gf, gl, cf, cb, explicit, add_force,
    )
    for k in range(3):
        coef[k] = ends[k]
    coef[3] = visc[0]
    coef[4] = visc[rows - 1]


def z_factor_kernel(visc_z, c, n, gf, gl, planes, cf, cb):
    depth = visc_z.shape[0]
    lo_wall = jnp.where(lax.axis_index("gz") == 0, HALF_Z, 0.0)
    hi_wall = jnp.where(lax.axis_index("gz") == lax.axis_size("gz") - 1, HALF_Z, 0.0)
    ends = factor(
        lambda i: visc_z[i], depth, HALF_Z, lo_wall * visc_z[0], hi_wall * visc_z[depth - 1],
        c, n, gf, gl, cf, cb,
    )
    for k in range(3):
        planes[k] = ends[k]


def to_lines(block):
    lines, width = block.shape
    turned = block.T.reshape(Y_CHUNKS, width // Y_CHUNKS, lines)
    return jnp.transpose(turned, (1, 0, 2))


def from_lines(block):
    length, chunks, lines = block.shape
    return jnp.transpose(block, (1, 0, 2)).reshape(length * chunks, lines).T


def y_factor_kernel(visc, c, n, gf, gl, al, ga, inv, nu, cf, cb):
    rows, depth, width = visc.shape
    length, chunks, lines = c.shape
    group = 128 // depth
    for g in range(rows // group):
        block = visc[g * group:(g + 1) * group].reshape(128, width)
        nu[:, :, g * 128:(g + 1) * 128] = to_lines(block)
    sub = iota((chunks, lines), 0)
    lo = jnp.where(sub == 0, HALF_Y * nu[0], 0.0)
    hi = jnp.where(sub == chunks - 1, HALF_Y * nu[length - 1], 0.0)
    first, across, last = factor(
        lambda i: nu[i], length, HALF_Y, lo, hi, c, n, gf, gl, cf, cb
    )
    inner = sub < chunks - 1
    e = HALF_Y * (nu[length - 1] + shift(nu[0], -1, 0))
    b = jnp.where(inner, 1.0 / e + last + shift(first, -1, 0), 1.0)
    o = jnp.where(sub < chunks - 2, shift(across, -1, 0), 0.0)
    s, k = 1, 0
    while s < chunks:
        r = 1.0 / b
        a = shift(o * r, s, 0)
        g = o * shift(r, -s, 0)
        al[k] = a
        ga[k] = g
        b = b - g * o - a * shift(o, s, 0)
        o = g * shift(o, -s, 0)
        s *= 2
        k += 1
    inv[...] = 1.0 / b


def x_solve_kernel(visc, vel, rhs0, c, n, coef, near, far, pair, cross, w, payload, edge_lo, edge_hi):
    rows, depth, width = visc.shape
    sub = iota((depth, width), 0)
    upper = lax.rem(lax.axis_index("gz"), 2)
    two = 2.0 * HALF_Z
    by_pair = two * (near[1] + pair[1]) * (pair[0] - near[0])
    by_cross = two * (far[1] + cross[1]) * (cross[0] - far[0])
    edge_lo[...] = jnp.where(upper == 0, by_cross, by_pair)
    edge_hi[...] = jnp.where(upper == 0, by_pair, by_cross)

    def rhs(i):
        at = pl.ds(i, 1)
        lo = jnp.where(sub == 0, edge_lo[at], 0.0)
        return rhs0[i] + jnp.where(sub == depth - 1, edge_hi[at], lo)

    d, u = block_solve(rhs, rows, c, n, w)
    payload[0] = d
    payload[1] = u
    for k in range(5):
        payload[2 + k] = coef[k]


def make_middle_kernel(parts_n):
    def kernel(*refs):
        parts = refs[:parts_n]
        (w, gf, gl, vel, cy, ny, gfy, gly, aly, gay, invy, cz, nz,
         dz, ends, slots, flux, src, sol, turned) = refs[parts_n:]
        rows, depth, width = w.shape
        me = lax.axis_index("gx")
        for k in range(parts_n):
            slots[jnp.bitwise_xor(me, k)] = parts[k][...]
        zero = jnp.zeros((depth, width), F32)
        flux[0] = zero
        flux[parts_n] = zero
        lower, source = [], []
        for f in range(parts_n - 1):
            e = HALF_X * (slots[f, 6] + slots[f + 1, 5])
            pivot = 1.0 / e + slots[f, 4] + slots[f + 1, 2]
            right = slots[f + 1, 0] - slots[f, 1]
            if f:
                pivot = pivot - slots[f, 3] * lower[-1]
                right = right + lower[-1] * source[-1]
            r = 1.0 / pivot
            lower.append(slots[f + 1, 3] * r)
            source.append(right)
            flux[f + 1] = right * r
        q = flux[parts_n - 1]
        for f in reversed(range(parts_n - 2)):
            q = flux[f + 1] + lower[f] * q
            flux[f + 1] = q
        q_left = flux[me]
        q_right = flux[me + 1]

        group = 128 // depth
        for g in range(rows // group):
            at = pl.ds(g * group, group)
            d = w[at] + q_right * gl[at] - q_left * gf[at] - 2.0 * vel[at]
            src[:, :, g * 128:(g + 1) * 128] = to_lines(d.reshape(128, width))

        length, chunks, lines = src.shape
        sub = iota((chunks, lines), 0)
        d, u = block_solve(lambda i: src[i], length, cy, ny, sol)
        q = jnp.where(sub < chunks - 1, shift(d, -1, 0) - u, 0.0)
        for k in range(aly.shape[0]):
            q = q + aly[k] * shift(q, 1 << k, 0) + gay[k] * shift(q, -(1 << k), 0)
        q = q * invy[...]
        ql = shift(q, 1, 0)
        for i in range(length):
            sol[i] = sol[i] + q * gly[i] - ql * gfy[i]
        for g in range(rows // group):
            block = from_lines(sol[:, :, g * 128:(g + 1) * 128])
            block = block.reshape(group, depth, width)
            turned[:, g * group:(g + 1) * group, :] = jnp.transpose(block, (1, 0, 2))
        d, u = block_solve(lambda i: turned[i], depth, cz, nz, dz)
        ends[0] = d
        ends[1] = u

    return kernel


def chip_factor_kernel(own, mate, near, far, pair, cross, pair_c, chip_c):
    is_low = lax.rem(lax.axis_index("gz"), 2) == 0
    low = [jnp.where(is_low, own[k], mate[k]) for k in range(3)]
    high = [jnp.where(is_low, mate[k], own[k]) for k in range(3)]
    mid_reach = 1.0 / (HALF_Z * (near[1] + pair[1]))
    end_reach = 1.0 / (HALF_Z * (far[1] + cross[1]))
    weight = 1.0 / (mid_reach + low[2] + high[0])
    pair_c[0] = weight
    pair_c[1] = low[1]
    pair_c[2] = high[1]
    chip_c[0] = low[0] - weight * low[1] * low[1] + jnp.where(is_low, end_reach, 0.0)
    chip_c[1] = weight * low[1] * high[1]
    chip_c[2] = high[2] - weight * high[1] * high[1] + jnp.where(is_low, 0.0, end_reach)


def pair_kernel(own, mate, pair_c, chip_ends, jump_out):
    is_low = lax.rem(lax.axis_index("gz"), 2) == 0
    low_last = jnp.where(is_low, own[1], mate[1])
    high_first = jnp.where(is_low, mate[0], own[0])
    jump = high_first - low_last
    q_mid = pair_c[0] * jump
    jump_out[...] = jump
    chip_ends[0] = jnp.where(is_low, own[0], mate[0]) + pair_c[1] * q_mid
    chip_ends[1] = jnp.where(is_low, mate[1], own[1]) - pair_c[2] * q_mid


def make_final_kernel(chips):
    def kernel(*refs):
        coefs, ends = refs[:chips], refs[chips:2 * chips]
        pair_c, jump, dz, gf, gl, out, c_at, d_at, flux, buf, sems = refs[2 * chips:]
        depth, rows, width = dz.shape
        parts = buf.shape[0]
        group = rows // parts
        chip = lax.div(lax.axis_index("gz"), 2)
        is_low = lax.rem(lax.axis_index("gz"), 2) == 0
        for k in range(chips):
            c_at[jnp.bitwise_xor(chip, k)] = coefs[k][...]
            d_at[jnp.bitwise_xor(chip, k)] = ends[k][...]
        zero = jnp.zeros((group, width), F32)
        copies = []
        for p in range(parts):
            at = slice(p * group, (p + 1) * group)
            flux[0] = zero
            flux[chips] = zero
            lower, right = [], None
            for f in range(chips - 1):
                pivot = c_at[f, 2, at] + c_at[f + 1, 0, at]
                source = d_at[f + 1, 0, at] - d_at[f, 1, at]
                if f:
                    pivot = pivot - c_at[f, 1, at] * lower[-1]
                    source = source + lower[-1] * right
                r = 1.0 / pivot
                lower.append(c_at[f + 1, 1, at] * r)
                right = source
                flux[f + 1] = source * r
            q = flux[chips - 1]
            for f in reversed(range(chips - 2)):
                q = flux[f + 1] + lower[f] * q
                flux[f + 1] = q
            left, right = flux[chip], flux[chip + 1]
            mid = pair_c[0, at] * (jump[at] + right * pair_c[2, at] + left * pair_c[1, at])
            q_left = jnp.where(is_low, left, mid)
            q_right = jnp.where(is_low, mid, right)
            d = dz[:, at] + q_right * gl[:, at] - q_left * gf[:, at]
            buf[p] = jnp.transpose(d, (1, 0, 2))
            copy = pltpu.make_async_copy(buf.at[p], out.at[pl.ds(p * group, group)], sems.at[p])
            copy.start()
            copies.append(copy)
        for copy in copies:
            copy.wait()

    return kernel


def local(velocity, viscosity, force):
    rows, depth, width = velocity.shape
    nx, nz = lax.axis_size("gx"), lax.axis_size("gz")
    chips = nz // 2
    volume = (rows, depth, width)
    zmajor = (depth, rows, width)
    lines = (width // Y_CHUNKS, Y_CHUNKS, rows * depth)
    size = rows * depth * width
    plane = (depth, width)
    slab = (rows, width)
    y_steps = (Y_CHUNKS - 1).bit_length()

    pair_route = [(i, i ^ 1) for i in range(nz)]
    cross_route = [(i, i + 1 if i % 2 else i - 1) for i in range(1, nz - 1)]

    def to_chip(k):
        return [(i, i ^ (2 * k)) for i in range(nz)]

    visc, vel = viscosity, velocity
    visc_z, near, far = call(
        turn_kernel, [zmajor, (2,) + slab, (2,) + slab], [VMEM, VMEM],
        [pltpu.VMEM(zmajor, F32)], size, 6 * size,
    )(visc, vel)
    pair = lax.ppermute(near, "gz", pair_route)
    cross = lax.ppermute(far, "gz", cross_route)

    c_z, n_z, gf_z, gl_z, planes = call(
        z_factor_kernel, [zmajor] * 4 + [(3,) + slab], [VMEM],
        [pltpu.VMEM(zmajor, F32)] * 2, 20 * size, 5 * size,
    )(visc_z)
    c_x, n_x, gf_x, gl_x, coef, rhs0 = call(
        x_factor_kernel, [volume] * 4 + [(5,) + plane, volume], [VMEM, VMEM, HBM],
        [pltpu.VMEM(volume, F32)] * 3 + [pltpu.SemaphoreType.DMA(())], 60 * size, 9 * size,
    )(visc, vel, force)
    c_y, n_y, gf_y, gl_y, al_y, ga_y, inv_y = call(
        y_factor_kernel, [lines] * 4 + [(y_steps,) + lines[1:]] * 2 + [lines[1:]], [VMEM],
        [pltpu.VMEM(lines, F32)] * 3, 30 * size, 6 * size,
    )(visc)

    mate_c = lax.ppermute(planes, "gz", pair_route)

    w, payload = call(
        x_solve_kernel, [volume, (7,) + plane], [VMEM] * 10,
        [pltpu.VMEM(slab, F32)] * 2, 20 * size, 6 * size,
    )(visc, vel, rhs0, c_x, n_x, coef, near, far, pair, cross)
    pair_c, chip_c = call(
        chip_factor_kernel, [(3,) + slab] * 2, [VMEM] * 6, (), size, size
    )(planes, mate_c, near, far, pair, cross)
    payload, chip_c = lax.optimization_barrier((payload, chip_c))
    parts = [payload] + [
        lax.ppermute(payload, "gx", [(i, i ^ k) for i in range(nx)]) for k in range(1, nx)
    ]
    coefs = [chip_c] + [lax.ppermute(chip_c, "gz", to_chip(k)) for k in range(1, chips)]

    w, *coefs = lax.optimization_barrier((w, *coefs))
    dz, ends = call(
        make_middle_kernel(nx), [zmajor, (2,) + slab], [VMEM] * (nx + 13),
        [pltpu.VMEM((nx, 7) + plane, F32), pltpu.VMEM((nx + 1,) + plane, F32),
         pltpu.VMEM(lines, F32), pltpu.VMEM(lines, F32), pltpu.VMEM(zmajor, F32)],
        60 * size, 14 * size,
    )(*parts, w, gf_x, gl_x, vel, c_y, n_y, gf_y, gl_y, al_y, ga_y, inv_y, c_z, n_z)

    mate = lax.ppermute(ends, "gz", pair_route)
    chip_ends, jump = call(pair_kernel, [(2,) + slab, slab], [VMEM] * 3, (), size, size)(
        ends, mate, pair_c
    )
    others = [chip_ends] + [lax.ppermute(chip_ends, "gz", to_chip(k)) for k in range(1, chips)]
    parts_out = 4
    group = (rows // parts_out, width)
    return call(
        make_final_kernel(chips), [volume], [VMEM] * (2 * chips + 5),
        [pltpu.VMEM((chips, 3) + slab, F32), pltpu.VMEM((chips, 2) + slab, F32),
         pltpu.VMEM((chips + 1,) + group, F32),
         pltpu.VMEM((parts_out, rows // parts_out, depth, width), F32),
         pltpu.SemaphoreType.DMA((parts_out,))],
        8 * size, 5 * size, [HBM],
    )(*coefs, *others, pair_c, jump, dz, gf_z, gl_z)[0]


def solution(mesh):
    return jax.shard_map(
        local,
        mesh=mesh,
        in_specs=(P("gx", "gz", None), P("gx", "gz", None), P("gx", "gz", None)),
        out_specs=P("gx", "gz", None),
        check_vma=False,
    )
```

```python
import jax
import jax.numpy as jnp
from jax import lax
from jax.experimental import pallas as pl
from jax.experimental.pallas import tpu as pltpu
from jax.sharding import PartitionSpec as P

HALF_X = 0.5 * 1600.0 * 0.5
HALF_Y = 0.5 * 0.5 * 0.5
HALF_Z = 0.5 * 400.0 * 0.5
Y_CHUNKS = 8

F32 = jnp.float32
VMEM = pl.BlockSpec(memory_space=pltpu.VMEM)
HBM = pl.BlockSpec(memory_space=pltpu.HBM)


def call(kernel, outs, ins, scratch=(), flops=0, touched=0, out_specs=None):
    return pl.pallas_call(
        kernel,
        out_shape=tuple(jax.ShapeDtypeStruct(s, F32) for s in outs),
        in_specs=ins,
        out_specs=tuple(out_specs or [VMEM] * len(outs)),
        scratch_shapes=list(scratch),
        compiler_params=pltpu.CompilerParams(vmem_limit_bytes=8 << 20),
        cost_estimate=pl.CostEstimate(
            flops=flops, bytes_accessed=4 * touched, transcendentals=0
        ),
    )


def iota(shape, dim):
    return lax.broadcasted_iota(jnp.int32, shape, dim)


def shift(x, s, axis):
    return pltpu.roll(x, s % x.shape[axis], axis)


def factor(nu, rows, half, lo_term, hi_term, c_out, n_out, gf_out, gl_out, cf, cb):
    mid = rows // 2
    s, t = 1.0 + lo_term, 1.0 + hi_term
    for i in range(rows - 1):
        e = half * (nu(i) + nu(i + 1))
        r = 1.0 / (s + e)
        c = e * r
        cf[i] = c
        if i < mid:
            c_out[i] = c
            n_out[i] = r
        s = 1.0 + c * s
        if i + 1 == mid:
            s_mid = s
        j = rows - 1 - i
        e = half * (nu(j) + nu(j - 1))
        r = 1.0 / (t + e)
        c = e * r
        cb[j] = c
        if j > mid:
            c_out[j] = c
            n_out[j] = r
        t = 1.0 + c * t
        if j - 1 == mid:
            t_mid = t
    n_out[mid] = 1.0 / (s_mid + t_mid - 1.0)
    gl = 1.0 / (s + hi_term)
    gf = 1.0 / (t + lo_term)
    ends = [gf, None, gl]
    gl_out[rows - 1] = gl
    gf_out[0] = gf
    for i in range(rows - 1):
        gl = cf[rows - 2 - i] * gl
        gl_out[rows - 2 - i] = gl
        gf = cb[i + 1] * gf
        gf_out[i + 1] = gf
    ends[1] = gl
    return ends


def block_solve(rhs, rows, c, n, out):
    mid = rows // 2
    d = rhs(0)
    out[0] = d
    u = rhs(rows - 1)
    out[rows - 1] = u
    for i in range(1, mid):
        d = rhs(i) + c[i - 1] * d
        out[i] = d
        j = rows - 1 - i
        if j > mid:
            u = rhs(j) + c[j + 1] * u
            out[j] = u
    d = (rhs(mid) + c[mid - 1] * d + c[mid + 1] * u) * n[mid]
    out[mid] = d
    u = d
    for i in range(1, mid + 1):
        j = mid - i
        d = out[j] * n[j] + c[j] * d
        out[j] = d
        j = mid + i
        if j < rows:
            u = out[j] * n[j] + c[j] * u
            out[j] = u
    return d, u


def turn_kernel(visc_hbm, vel_hbm, visc, vel, visc_z, near, far, vel_z, sems):
    rows, depth, width = visc.shape
    upper = lax.rem(lax.axis_index("gz"), 2)
    near_at = (1 - upper) * (depth - 1)
    far_at = upper * (depth - 1)
    pieces = sems.shape[1]
    piece = rows // pieces
    copies = [
        [
            pltpu.make_async_copy(
                src.at[pl.ds(p * piece, piece)], dst.at[pl.ds(p * piece, piece)], sems.at[k, p]
            )
            for p in range(pieces)
        ]
        for k, (src, dst) in enumerate(((vel_hbm, vel), (visc_hbm, visc)))
    ]
    for p in range(pieces):
        for k in range(2):
            copies[k][p].start()
    for p in range(pieces):
        at = slice(p * piece, (p + 1) * piece)
        for k, (src, turned) in enumerate(((vel, vel_z), (visc, visc_z))):
            copies[k][p].wait()
            turned[:, at] = jnp.transpose(src[at], (1, 0, 2))
            near[k, at] = turned[near_at, at]
            far[k, at] = turned[far_at, at]


def x_factor_kernel(visc, vel, force_hbm, c, n, gf, gl, coef, rhs, cf, cb, force, sem):
    rows, depth, width = visc.shape
    copy = pltpu.make_async_copy(force_hbm, force, sem)
    copy.start()
    lo_wall = jnp.where(lax.axis_index("gx") == 0, HALF_X, 0.0)
    hi_wall = jnp.where(lax.axis_index("gx") == lax.axis_size("gx") - 1, HALF_X, 0.0)
    ends = factor(
        lambda i: visc[i], rows, HALF_X, lo_wall * visc[0], hi_wall * visc[rows - 1],
        c, n, gf, gl, cf, cb,
    )
    for k in range(3):
        coef[k] = ends[k]
    coef[3] = visc[0]
    coef[4] = visc[rows - 1]
    block = min(rows, 16)
    lane = iota((block, depth, width), 2)
    sub = iota((block, depth, width), 1)
    copy.wait()
    for i in range(0, rows, block):
        at = slice(i, i + block)
        v = vel[at]
        nu = visc[at]
        vn = jnp.where(lane == width - 1, 0.0, shift(v, -1, 2))
        nn = jnp.where(lane == width - 1, 0.0, shift(nu, -1, 2))
        fy = (2.0 * HALF_Y) * (nu + nn) * (vn - v)
        fl = jnp.where(lane == 0, (2.0 * HALF_Y) * nu * v, shift(fy, 1, 2))
        fz = (2.0 * HALF_Z) * (nu + shift(nu, -1, 1)) * (shift(v, -1, 1) - v)
        fz = jnp.where(sub == depth - 1, 0.0, fz)
        rhs[at] = force[at] + 2.0 * v + (fy - fl) + (fz - shift(fz, 1, 1))


def split_rows(source, keep, give):
    half = keep.shape[1]
    upper = lax.rem(lax.axis_index("gz"), 2)
    keep[...] = source[:, pl.ds(pl.multiple_of(upper * half, half), half)]
    give[...] = source[:, pl.ds(pl.multiple_of((1 - upper) * half, half), half)]


def z_factor_kernel(visc_z, c, n, gf, gl, keep, give, cf, cb, planes):
    depth = visc_z.shape[0]
    lo_wall = jnp.where(lax.axis_index("gz") == 0, HALF_Z, 0.0)
    hi_wall = jnp.where(lax.axis_index("gz") == lax.axis_size("gz") - 1, HALF_Z, 0.0)
    ends = factor(
        lambda i: visc_z[i], depth, HALF_Z, lo_wall * visc_z[0], hi_wall * visc_z[depth - 1],
        c, n, gf, gl, cf, cb,
    )
    for k in range(3):
        planes[k] = ends[k]
    split_rows(planes, keep, give)


def to_lines(block):
    lines, width = block.shape
    turned = block.T.reshape(Y_CHUNKS, width // Y_CHUNKS, lines)
    return jnp.transpose(turned, (1, 0, 2))


def from_lines(block):
    length, chunks, lines = block.shape
    return jnp.transpose(block, (1, 0, 2)).reshape(length * chunks, lines).T


def y_factor_kernel(visc, c, n, gf, gl, al, ga, inv, nu, cf, cb):
    rows, depth, width = visc.shape
    length, chunks, lines = c.shape
    group = 128 // depth
    for g in range(rows // group):
        block = visc[g * group:(g + 1) * group].reshape(128, width)
        nu[:, :, g * 128:(g + 1) * 128] = to_lines(block)
    sub = iota((chunks, lines), 0)
    lo = jnp.where(sub == 0, HALF_Y * nu[0], 0.0)
    hi = jnp.where(sub == chunks - 1, HALF_Y * nu[length - 1], 0.0)
    first, across, last = factor(
        lambda i: nu[i], length, HALF_Y, lo, hi, c, n, gf, gl, cf, cb
    )
    inner = sub < chunks - 1
    e = HALF_Y * (nu[length - 1] + shift(nu[0], -1, 0))
    b = jnp.where(inner, 1.0 / e + last + shift(first, -1, 0), 1.0)
    o = jnp.where(sub < chunks - 2, shift(across, -1, 0), 0.0)
    s, k = 1, 0
    while s < chunks:
        r = 1.0 / b
        a = shift(o * r, s, 0)
        g = o * shift(r, -s, 0)
        al[k] = a
        ga[k] = g
        b = b - g * o - a * shift(o, s, 0)
        o = g * shift(o, -s, 0)
        s *= 2
        k += 1
    inv[...] = 1.0 / b


def x_solve_kernel(visc, vel, rhs0, c, n, coef, near, far, pair, cross, w, payload, edge_lo, edge_hi):
    rows, depth, width = visc.shape
    sub = iota((depth, width), 0)
    upper = lax.rem(lax.axis_index("gz"), 2)
    two = 2.0 * HALF_Z
    by_pair = two * (near[1] + pair[1]) * (pair[0] - near[0])
    by_cross = two * (far[1] + cross[1]) * (cross[0] - far[0])
    edge_lo[...] = jnp.where(upper == 0, by_cross, by_pair)
    edge_hi[...] = jnp.where(upper == 0, by_pair, by_cross)

    def rhs(i):
        at = pl.ds(i, 1)
        lo = jnp.where(sub == 0, edge_lo[at], 0.0)
        return rhs0[i] + jnp.where(sub == depth - 1, edge_hi[at], lo)

    d, u = block_solve(rhs, rows, c, n, w)
    payload[0] = d
    payload[1] = u
    for k in range(5):
        payload[2 + k] = coef[k]


def make_middle_kernel(parts_n):
    def kernel(*refs):
        parts = refs[:parts_n]
        (w, gf, gl, vel, cy, ny, gfy, gly, aly, gay, invy, cz, nz,
         dz, keep, give, slots, flux, src, sol, turned, ends) = refs[parts_n:]
        rows, depth, width = w.shape
        me = lax.axis_index("gx")
        for k in range(parts_n):
            slots[jnp.bitwise_xor(me, k)] = parts[k][...]
        zero = jnp.zeros((depth, width), F32)
        flux[0] = zero
        flux[parts_n] = zero
        lower, source = [], []
        for f in range(parts_n - 1):
            e = HALF_X * (slots[f, 6] + slots[f + 1, 5])
            pivot = 1.0 / e + slots[f, 4] + slots[f + 1, 2]
            right = slots[f + 1, 0] - slots[f, 1]
            if f:
                pivot = pivot - slots[f, 3] * lower[-1]
                right = right + lower[-1] * source[-1]
            r = 1.0 / pivot
            lower.append(slots[f + 1, 3] * r)
            source.append(right)
            flux[f + 1] = right * r
        q = flux[parts_n - 1]
        for f in reversed(range(parts_n - 2)):
            q = flux[f + 1] + lower[f] * q
            flux[f + 1] = q
        q_left = flux[me]
        q_right = flux[me + 1]

        group = 128 // depth
        for g in range(rows // group):
            at = pl.ds(g * group, group)
            d = w[at] + q_right * gl[at] - q_left * gf[at] - 2.0 * vel[at]
            src[:, :, g * 128:(g + 1) * 128] = to_lines(d.reshape(128, width))

        length, chunks, lines = src.shape
        sub = iota((chunks, lines), 0)
        d, u = block_solve(lambda i: src[i], length, cy, ny, sol)
        q = jnp.where(sub < chunks - 1, shift(d, -1, 0) - u, 0.0)
        for k in range(aly.shape[0]):
            q = q + aly[k] * shift(q, 1 << k, 0) + gay[k] * shift(q, -(1 << k), 0)
        q = q * invy[...]
        ql = shift(q, 1, 0)
        for i in range(length):
            sol[i] = sol[i] + q * gly[i] - ql * gfy[i]
        for g in range(rows // group):
            block = from_lines(sol[:, :, g * 128:(g + 1) * 128])
            block = block.reshape(group, depth, width)
            turned[:, g * group:(g + 1) * group, :] = jnp.transpose(block, (1, 0, 2))
        d, u = block_solve(lambda i: turned[i], depth, cz, nz, dz)
        ends[0] = d
        ends[1] = u
        split_rows(ends, keep, give)

    return kernel


def chip_factor_kernel(own, mate, near, far, pair, cross, pair_c, chip_c):
    half = own.shape[1]
    upper = lax.rem(lax.axis_index("gz"), 2)
    at = pl.ds(pl.multiple_of(upper * half, half), half)
    is_low = upper == 0
    low = [jnp.where(is_low, own[k], mate[k]) for k in range(3)]
    high = [jnp.where(is_low, mate[k], own[k]) for k in range(3)]
    mid_reach = 1.0 / (HALF_Z * (near[1, at] + pair[1, at]))
    end_reach = 1.0 / (HALF_Z * (far[1, at] + cross[1, at]))
    weight = 1.0 / (mid_reach + low[2] + high[0])
    pair_c[0] = weight
    pair_c[1] = low[1]
    pair_c[2] = high[1]
    chip_c[0] = low[0] - weight * low[1] * low[1] + jnp.where(is_low, end_reach, 0.0)
    chip_c[1] = weight * low[1] * high[1]
    chip_c[2] = high[2] - weight * high[1] * high[1] + jnp.where(is_low, 0.0, end_reach)


def pair_kernel(own, mate, pair_c, chip_c, payload, jump_out):
    is_low = lax.rem(lax.axis_index("gz"), 2) == 0
    low_last = jnp.where(is_low, own[1], mate[1])
    high_first = jnp.where(is_low, mate[0], own[0])
    jump = high_first - low_last
    q_mid = pair_c[0] * jump
    jump_out[...] = jump
    payload[0] = jnp.where(is_low, own[0], mate[0]) + pair_c[1] * q_mid
    payload[1] = jnp.where(is_low, mate[1], own[1]) - pair_c[2] * q_mid
    for k in range(3):
        payload[2 + k] = chip_c[k]


def make_flux_kernel(chips):
    def kernel(*refs):
        parts = refs[:chips]
        pair_c, jump, mine, theirs, slots, flux = refs[chips:]
        chip = lax.div(lax.axis_index("gz"), 2)
        is_low = lax.rem(lax.axis_index("gz"), 2) == 0
        for k in range(chips):
            slots[jnp.bitwise_xor(chip, k)] = parts[k][...]
        flux[0] = jnp.zeros_like(jump)
        flux[chips] = jnp.zeros_like(jump)
        lower, right = [], None
        for f in range(chips - 1):
            pivot = slots[f, 4] + slots[f + 1, 2]
            source = slots[f + 1, 0] - slots[f, 1]
            if f:
                pivot = pivot - slots[f, 3] * lower[-1]
                source = source + lower[-1] * right
            r = 1.0 / pivot
            lower.append(slots[f + 1, 3] * r)
            right = source
            flux[f + 1] = source * r
        q = flux[chips - 1]
        for f in reversed(range(chips - 2)):
            q = flux[f + 1] + lower[f] * q
            flux[f + 1] = q
        left, right = flux[chip], flux[chip + 1]
        mid = pair_c[0] * (jump[...] + right * pair_c[2] + left * pair_c[1])
        mine[0] = jnp.where(is_low, left, mid)
        mine[1] = jnp.where(is_low, mid, right)
        theirs[0] = jnp.where(is_low, mid, left)
        theirs[1] = jnp.where(is_low, right, mid)

    return kernel


def final_kernel(mine, got, dz, gf, gl, out, buf, sems):
    depth, rows, width = dz.shape
    parts = buf.shape[0]
    group = rows // parts
    half = rows // 2
    is_low = lax.rem(lax.axis_index("gz"), 2) == 0
    copies = []
    for p in range(parts):
        at = slice(p * group, (p + 1) * group)
        top = p * group < half
        inside = slice(p * group % half, p * group % half + group)
        own_rows = is_low if top else jnp.logical_not(is_low)
        q_left = jnp.where(own_rows, mine[0, inside], got[0, inside])
        q_right = jnp.where(own_rows, mine[1, inside], got[1, inside])
        d = dz[:, at] + q_right * gl[:, at] - q_left * gf[:, at]
        buf[p] = jnp.transpose(d, (1, 0, 2))
        copy = pltpu.make_async_copy(buf.at[p], out.at[pl.ds(p * group, group)], sems.at[p])
        copy.start()
        copies.append(copy)
    for copy in copies:
        copy.wait()


def local(velocity, viscosity, force):
    rows, depth, width = velocity.shape
    nx, nz = lax.axis_size("gx"), lax.axis_size("gz")
    chips = nz // 2
    volume = (rows, depth, width)
    zmajor = (depth, rows, width)
    lines = (width // Y_CHUNKS, Y_CHUNKS, rows * depth)
    size = rows * depth * width
    plane = (depth, width)
    slab = (rows, width)
    y_steps = (Y_CHUNKS - 1).bit_length()

    pair_route = [(i, i ^ 1) for i in range(nz)]
    cross_route = [(i, i + 1 if i % 2 else i - 1) for i in range(1, nz - 1)]

    def to_chip(k):
        return [(i, i ^ (2 * k)) for i in range(nz)]

    pieces = 4
    visc, vel, visc_z, near, far = call(
        turn_kernel, [volume, volume, zmajor, (2,) + slab, (2,) + slab], [HBM, HBM],
        [pltpu.VMEM(zmajor, F32), pltpu.SemaphoreType.DMA((2, pieces))], size, 6 * size,
    )(
        pltpu.with_memory_space_constraint(viscosity, pltpu.HBM),
        pltpu.with_memory_space_constraint(velocity, pltpu.HBM),
    )
    pair = lax.ppermute(near, "gz", pair_route)
    cross = lax.ppermute(far, "gz", cross_route)

    half = (rows // 2, width)
    c_z, n_z, gf_z, gl_z, planes, give_c = call(
        z_factor_kernel, [zmajor] * 4 + [(3,) + half] * 2, [VMEM],
        [pltpu.VMEM(zmajor, F32)] * 2 + [pltpu.VMEM((3,) + slab, F32)], 20 * size, 5 * size,
    )(visc_z)
    c_x, n_x, gf_x, gl_x, coef, rhs0 = call(
        x_factor_kernel, [volume] * 4 + [(5,) + plane, volume], [VMEM, VMEM, HBM],
        [pltpu.VMEM(volume, F32)] * 3 + [pltpu.SemaphoreType.DMA(())], 60 * size, 9 * size,
    )(visc, vel, force)
    c_y, n_y, gf_y, gl_y, al_y, ga_y, inv_y = call(
        y_factor_kernel, [lines] * 4 + [(y_steps,) + lines[1:]] * 2 + [lines[1:]], [VMEM],
        [pltpu.VMEM(lines, F32)] * 3, 30 * size, 6 * size,
    )(visc)

    mate_c = lax.ppermute(give_c, "gz", pair_route)

    w, payload = call(
        x_solve_kernel, [volume, (7,) + plane], [VMEM] * 10,
        [pltpu.VMEM(slab, F32)] * 2, 20 * size, 6 * size,
    )(visc, vel, rhs0, c_x, n_x, coef, near, far, pair, cross)
    pair_c, chip_c = call(
        chip_factor_kernel, [(3,) + half] * 2, [VMEM] * 6, (), size, size
    )(planes, mate_c, near, far, pair, cross)
    parts = [payload] + [
        lax.ppermute(payload, "gx", [(i, i ^ k) for i in range(nx)]) for k in range(1, nx)
    ]
    dz, keep, give = call(
        make_middle_kernel(nx), [zmajor, (2,) + half, (2,) + half], [VMEM] * (nx + 13),
        [pltpu.VMEM((nx, 7) + plane, F32), pltpu.VMEM((nx + 1,) + plane, F32),
         pltpu.VMEM(lines, F32), pltpu.VMEM(lines, F32), pltpu.VMEM(zmajor, F32),
         pltpu.VMEM((2,) + slab, F32)],
        60 * size, 14 * size,
    )(*parts, w, gf_x, gl_x, vel, c_y, n_y, gf_y, gl_y, al_y, ga_y, inv_y, c_z, n_z)

    mate = lax.ppermute(give, "gz", pair_route)
    chip_ends, jump = call(pair_kernel, [(5,) + half, half], [VMEM] * 4, (), size, size)(
        keep, mate, pair_c, chip_c
    )
    others = [chip_ends] + [lax.ppermute(chip_ends, "gz", to_chip(k)) for k in range(1, chips)]
    mine, theirs = call(
        make_flux_kernel(chips), [(2,) + half] * 2, [VMEM] * (chips + 2),
        [pltpu.VMEM((chips, 5) + half, F32), pltpu.VMEM((chips + 1,) + half, F32)], size, size,
    )(*others, pair_c, jump)
    got = lax.ppermute(theirs, "gz", pair_route)
    return call(
        final_kernel, [volume], [VMEM] * 5,
        [pltpu.VMEM((4, rows // 4, depth, width), F32), pltpu.SemaphoreType.DMA((4,))],
        4 * size, 4 * size, [HBM],
    )(mine, got, dz, gf_z, gl_z)[0]


def solution(mesh):
    return jax.shard_map(
        local,
        mesh=mesh,
        in_specs=(P("gx", "gz", None), P("gx", "gz", None), P("gx", "gz", None)),
        out_specs=P("gx", "gz", None),
        check_vma=False,
    )
```

```python
import jax
import jax.numpy as jnp
from jax import lax
from jax.experimental import pallas as pl
from jax.experimental.pallas import tpu as pltpu
from jax.sharding import PartitionSpec as P

HALF_X = 0.5 * 1600.0 * 0.5
HALF_Y = 0.5 * 0.5 * 0.5
HALF_Z = 0.5 * 400.0 * 0.5
Y_CHUNKS = 8

F32 = jnp.float32
VMEM = pl.BlockSpec(memory_space=pltpu.VMEM)
HBM = pl.BlockSpec(memory_space=pltpu.HBM)


def call(kernel, outs, ins, scratch=(), flops=0, touched=0, out_specs=None):
    return pl.pallas_call(
        kernel,
        out_shape=tuple(jax.ShapeDtypeStruct(s, F32) for s in outs),
        in_specs=ins,
        out_specs=tuple(out_specs or [VMEM] * len(outs)),
        scratch_shapes=list(scratch),
        compiler_params=pltpu.CompilerParams(vmem_limit_bytes=8 << 20),
        cost_estimate=pl.CostEstimate(
            flops=flops, bytes_accessed=4 * touched, transcendentals=0
        ),
    )


def iota(shape, dim):
    return lax.broadcasted_iota(jnp.int32, shape, dim)


def shift(x, s, axis):
    return pltpu.roll(x, s % x.shape[axis], axis)


def factor(nu, rows, half, lo_term, hi_term, c_out, n_out, gf_out, gl_out, cf, cb):
    mid = rows // 2
    s, t = 1.0 + lo_term, 1.0 + hi_term
    for i in range(rows - 1):
        e = half * (nu(i) + nu(i + 1))
        r = 1.0 / (s + e)
        c = e * r
        cf[i] = c
        if i < mid:
            c_out[i] = c
            n_out[i] = r
        s = 1.0 + c * s
        if i + 1 == mid:
            s_mid = s
        j = rows - 1 - i
        e = half * (nu(j) + nu(j - 1))
        r = 1.0 / (t + e)
        c = e * r
        cb[j] = c
        if j > mid:
            c_out[j] = c
            n_out[j] = r
        t = 1.0 + c * t
        if j - 1 == mid:
            t_mid = t
    n_out[mid] = 1.0 / (s_mid + t_mid - 1.0)
    gl = 1.0 / (s + hi_term)
    gf = 1.0 / (t + lo_term)
    ends = [gf, None, gl]
    gl_out[rows - 1] = gl
    gf_out[0] = gf
    for i in range(rows - 1):
        gl = cf[rows - 2 - i] * gl
        gl_out[rows - 2 - i] = gl
        gf = cb[i + 1] * gf
        gf_out[i + 1] = gf
    ends[1] = gl
    return ends


def block_solve(rhs, rows, c, n, out):
    mid = rows // 2
    d = rhs(0)
    out[0] = d
    u = rhs(rows - 1)
    out[rows - 1] = u
    for i in range(1, mid):
        d = rhs(i) + c[i - 1] * d
        out[i] = d
        j = rows - 1 - i
        if j > mid:
            u = rhs(j) + c[j + 1] * u
            out[j] = u
    d = (rhs(mid) + c[mid - 1] * d + c[mid + 1] * u) * n[mid]
    out[mid] = d
    u = d
    for i in range(1, mid + 1):
        j = mid - i
        d = out[j] * n[j] + c[j] * d
        out[j] = d
        j = mid + i
        if j < rows:
            u = out[j] * n[j] + c[j] * u
            out[j] = u
    return d, u


def far_kernel(visc_hbm, vel_hbm, far, sems):
    rows, depth, width = visc_hbm.shape
    at = lax.rem(lax.axis_index("gz"), 2) * (depth - 1)
    copies = [
        pltpu.make_async_copy(src.at[:, at], far.at[k], sems.at[k])
        for k, src in enumerate((vel_hbm, visc_hbm))
    ]
    for copy in copies:
        copy.start()
    for copy in copies:
        copy.wait()


def load_kernel(visc_hbm, vel_hbm, visc, vel, visc_z, near, vel_z, sems):
    rows, depth, width = visc.shape
    near_at = (1 - lax.rem(lax.axis_index("gz"), 2)) * (depth - 1)
    copies = [
        pltpu.make_async_copy(src, dst, sems.at[k])
        for k, (src, dst) in enumerate(((vel_hbm, vel), (visc_hbm, visc)))
    ]
    for copy in copies:
        copy.start()
    for k, (src, turned) in enumerate(((vel, vel_z), (visc, visc_z))):
        copies[k].wait()
        turned[...] = jnp.transpose(src[...], (1, 0, 2))
        near[k] = turned[near_at]


def x_factor_kernel(visc, vel, force_hbm, c, n, gf, gl, coef, rhs, cf, cb, force, sem):
    rows, depth, width = visc.shape
    copy = pltpu.make_async_copy(force_hbm, force, sem)
    copy.start()
    lo_wall = jnp.where(lax.axis_index("gx") == 0, HALF_X, 0.0)
    hi_wall = jnp.where(lax.axis_index("gx") == lax.axis_size("gx") - 1, HALF_X, 0.0)
    ends = factor(
        lambda i: visc[i], rows, HALF_X, lo_wall * visc[0], hi_wall * visc[rows - 1],
        c, n, gf, gl, cf, cb,
    )
    for k in range(3):
        coef[k] = ends[k]
    coef[3] = visc[0]
    coef[4] = visc[rows - 1]
    block = min(rows, 16)
    lane = iota((block, depth, width), 2)
    sub = iota((block, depth, width), 1)
    copy.wait()
    for i in range(0, rows, block):
        at = slice(i, i + block)
        v = vel[at]
        nu = visc[at]
        vn = jnp.where(lane == width - 1, 0.0, shift(v, -1, 2))
        nn = jnp.where(lane == width - 1, 0.0, shift(nu, -1, 2))
        fy = (2.0 * HALF_Y) * (nu + nn) * (vn - v)
        fl = jnp.where(lane == 0, (2.0 * HALF_Y) * nu * v, shift(fy, 1, 2))
        fz = (2.0 * HALF_Z) * (nu + shift(nu, -1, 1)) * (shift(v, -1, 1) - v)
        fz = jnp.where(sub == depth - 1, 0.0, fz)
        rhs[at] = force[at] + 2.0 * v + (fy - fl) + (fz - shift(fz, 1, 1))


def split_rows(source, keep, give):
    half = keep.shape[1]
    upper = lax.rem(lax.axis_index("gz"), 2)
    keep[...] = source[:, pl.ds(pl.multiple_of(upper * half, half), half)]
    give[...] = source[:, pl.ds(pl.multiple_of((1 - upper) * half, half), half)]


def z_factor_kernel(visc_z, c, n, gf, gl, keep, give, cf, cb, planes):
    depth = visc_z.shape[0]
    lo_wall = jnp.where(lax.axis_index("gz") == 0, HALF_Z, 0.0)
    hi_wall = jnp.where(lax.axis_index("gz") == lax.axis_size("gz") - 1, HALF_Z, 0.0)
    ends = factor(
        lambda i: visc_z[i], depth, HALF_Z, lo_wall * visc_z[0], hi_wall * visc_z[depth - 1],
        c, n, gf, gl, cf, cb,
    )
    for k in range(3):
        planes[k] = ends[k]
    split_rows(planes, keep, give)


def to_lines(block):
    lines, width = block.shape
    turned = block.T.reshape(Y_CHUNKS, width // Y_CHUNKS, lines)
    return jnp.transpose(turned, (1, 0, 2))


def from_lines(block):
    length, chunks, lines = block.shape
    return jnp.transpose(block, (1, 0, 2)).reshape(length * chunks, lines).T


def y_factor_kernel(visc, c, n, gf, gl, al, ga, inv, nu, cf, cb):
    rows, depth, width = visc.shape
    length, chunks, lines = c.shape
    group = 128 // depth
    for g in range(rows // group):
        block = visc[g * group:(g + 1) * group].reshape(128, width)
        nu[:, :, g * 128:(g + 1) * 128] = to_lines(block)
    sub = iota((chunks, lines), 0)
    lo = jnp.where(sub == 0, HALF_Y * nu[0], 0.0)
    hi = jnp.where(sub == chunks - 1, HALF_Y * nu[length - 1], 0.0)
    first, across, last = factor(
        lambda i: nu[i], length, HALF_Y, lo, hi, c, n, gf, gl, cf, cb
    )
    inner = sub < chunks - 1
    e = HALF_Y * (nu[length - 1] + shift(nu[0], -1, 0))
    b = jnp.where(inner, 1.0 / e + last + shift(first, -1, 0), 1.0)
    o = jnp.where(sub < chunks - 2, shift(across, -1, 0), 0.0)
    s, k = 1, 0
    while s < chunks:
        r = 1.0 / b
        a = shift(o * r, s, 0)
        g = o * shift(r, -s, 0)
        al[k] = a
        ga[k] = g
        b = b - g * o - a * shift(o, s, 0)
        o = g * shift(o, -s, 0)
        s *= 2
        k += 1
    inv[...] = 1.0 / b


def outer_edge_kernel(far, cross, edge):
    edge[...] = (2.0 * HALF_Z) * (far[1] + cross[1]) * (cross[0] - far[0])


def x_solve_kernel(visc, vel, rhs0, c, n, coef, near, pair, by_cross_ref, w, payload, edge_lo, edge_hi):
    rows, depth, width = visc.shape
    sub = iota((depth, width), 0)
    upper = lax.rem(lax.axis_index("gz"), 2)
    two = 2.0 * HALF_Z
    by_pair = two * (near[1] + pair[1]) * (pair[0] - near[0])
    by_cross = by_cross_ref[...]
    edge_lo[...] = jnp.where(upper == 0, by_cross, by_pair)
    edge_hi[...] = jnp.where(upper == 0, by_pair, by_cross)

    def rhs(i):
        at = pl.ds(i, 1)
        lo = jnp.where(sub == 0, edge_lo[at], 0.0)
        return rhs0[i] + jnp.where(sub == depth - 1, edge_hi[at], lo)

    d, u = block_solve(rhs, rows, c, n, w)
    payload[0] = d
    payload[1] = u
    for k in range(5):
        payload[2 + k] = coef[k]


def make_middle_kernel(parts_n):
    def kernel(*refs):
        parts = refs[:parts_n]
        (w, gf, gl, vel, cy, ny, gfy, gly, aly, gay, invy, cz, nz,
         dz, keep, give, slots, flux, src, sol, turned, ends) = refs[parts_n:]
        rows, depth, width = w.shape
        me = lax.axis_index("gx")
        for k in range(parts_n):
            slots[jnp.bitwise_xor(me, k)] = parts[k][...]
        zero = jnp.zeros((depth, width), F32)
        flux[0] = zero
        flux[parts_n] = zero
        lower, source = [], []
        for f in range(parts_n - 1):
            e = HALF_X * (slots[f, 6] + slots[f + 1, 5])
            pivot = 1.0 / e + slots[f, 4] + slots[f + 1, 2]
            right = slots[f + 1, 0] - slots[f, 1]
            if f:
                pivot = pivot - slots[f, 3] * lower[-1]
                right = right + lower[-1] * source[-1]
            r = 1.0 / pivot
            lower.append(slots[f + 1, 3] * r)
            source.append(right)
            flux[f + 1] = right * r
        q = flux[parts_n - 1]
        for f in reversed(range(parts_n - 2)):
            q = flux[f + 1] + lower[f] * q
            flux[f + 1] = q
        q_left = flux[me]
        q_right = flux[me + 1]

        group = 128 // depth
        for g in range(rows // group):
            at = pl.ds(g * group, group)
            d = w[at] + q_right * gl[at] - q_left * gf[at] - 2.0 * vel[at]
            src[:, :, g * 128:(g + 1) * 128] = to_lines(d.reshape(128, width))

        length, chunks, lines = src.shape
        sub = iota((chunks, lines), 0)
        d, u = block_solve(lambda i: src[i], length, cy, ny, sol)
        q = jnp.where(sub < chunks - 1, shift(d, -1, 0) - u, 0.0)
        for k in range(aly.shape[0]):
            q = q + aly[k] * shift(q, 1 << k, 0) + gay[k] * shift(q, -(1 << k), 0)
        q = q * invy[...]
        ql = shift(q, 1, 0)
        for i in range(length):
            sol[i] = sol[i] + q * gly[i] - ql * gfy[i]
        for g in range(rows // group):
            block = from_lines(sol[:, :, g * 128:(g + 1) * 128])
            block = block.reshape(group, depth, width)
            turned[:, g * group:(g + 1) * group, :] = jnp.transpose(block, (1, 0, 2))
        d, u = block_solve(lambda i: turned[i], depth, cz, nz, dz)
        ends[0] = d
        ends[1] = u
        split_rows(ends, keep, give)

    return kernel


def chip_factor_kernel(own, mate, near, far, pair, cross, pair_c, chip_c):
    half = own.shape[1]
    upper = lax.rem(lax.axis_index("gz"), 2)
    at = pl.ds(pl.multiple_of(upper * half, half), half)
    is_low = upper == 0
    low = [jnp.where(is_low, own[k], mate[k]) for k in range(3)]
    high = [jnp.where(is_low, mate[k], own[k]) for k in range(3)]
    mid_reach = 1.0 / (HALF_Z * (near[1, at] + pair[1, at]))
    end_reach = 1.0 / (HALF_Z * (far[1, at] + cross[1, at]))
    weight = 1.0 / (mid_reach + low[2] + high[0])
    pair_c[0] = weight
    pair_c[1] = low[1]
    pair_c[2] = high[1]
    chip_c[0] = low[0] - weight * low[1] * low[1] + jnp.where(is_low, end_reach, 0.0)
    chip_c[1] = weight * low[1] * high[1]
    chip_c[2] = high[2] - weight * high[1] * high[1] + jnp.where(is_low, 0.0, end_reach)


def pair_kernel(own, mate, pair_c, chip_c, payload, jump_out):
    is_low = lax.rem(lax.axis_index("gz"), 2) == 0
    low_last = jnp.where(is_low, own[1], mate[1])
    high_first = jnp.where(is_low, mate[0], own[0])
    jump = high_first - low_last
    q_mid = pair_c[0] * jump
    jump_out[...] = jump
    payload[0] = jnp.where(is_low, own[0], mate[0]) + pair_c[1] * q_mid
    payload[1] = jnp.where(is_low, mate[1], own[1]) - pair_c[2] * q_mid
    for k in range(3):
        payload[2 + k] = chip_c[k]


def make_flux_kernel(chips):
    def kernel(*refs):
        parts = refs[:chips]
        pair_c, jump, mine, theirs, slots, flux = refs[chips:]
        chip = lax.div(lax.axis_index("gz"), 2)
        is_low = lax.rem(lax.axis_index("gz"), 2) == 0
        for k in range(chips):
            slots[jnp.bitwise_xor(chip, k)] = parts[k][...]
        flux[0] = jnp.zeros_like(jump)
        flux[chips] = jnp.zeros_like(jump)
        lower, right = [], None
        for f in range(chips - 1):
            pivot = slots[f, 4] + slots[f + 1, 2]
            source = slots[f + 1, 0] - slots[f, 1]
            if f:
                pivot = pivot - slots[f, 3] * lower[-1]
                source = source + lower[-1] * right
            r = 1.0 / pivot
            lower.append(slots[f + 1, 3] * r)
            right = source
            flux[f + 1] = source * r
        q = flux[chips - 1]
        for f in reversed(range(chips - 2)):
            q = flux[f + 1] + lower[f] * q
            flux[f + 1] = q
        left, right = flux[chip], flux[chip + 1]
        mid = pair_c[0] * (jump[...] + right * pair_c[2] + left * pair_c[1])
        mine[0] = jnp.where(is_low, left, mid)
        mine[1] = jnp.where(is_low, mid, right)
        theirs[0] = jnp.where(is_low, mid, left)
        theirs[1] = jnp.where(is_low, right, mid)

    return kernel


def final_kernel(mine, got, dz, gf, gl, out, buf, sems):
    depth, rows, width = dz.shape
    parts = buf.shape[0]
    group = rows // parts
    half = rows // 2
    is_low = lax.rem(lax.axis_index("gz"), 2) == 0
    copies = []
    for p in range(parts):
        at = slice(p * group, (p + 1) * group)
        top = p * group < half
        inside = slice(p * group % half, p * group % half + group)
        own_rows = is_low if top else jnp.logical_not(is_low)
        q_left = jnp.where(own_rows, mine[0, inside], got[0, inside])
        q_right = jnp.where(own_rows, mine[1, inside], got[1, inside])
        d = dz[:, at] + q_right * gl[:, at] - q_left * gf[:, at]
        buf[p] = jnp.transpose(d, (1, 0, 2))
        copy = pltpu.make_async_copy(buf.at[p], out.at[pl.ds(p * group, group)], sems.at[p])
        copy.start()
        copies.append(copy)
    for copy in copies:
        copy.wait()


def local(velocity, viscosity, force):
    rows, depth, width = velocity.shape
    nx, nz = lax.axis_size("gx"), lax.axis_size("gz")
    chips = nz // 2
    volume = (rows, depth, width)
    zmajor = (depth, rows, width)
    lines = (width // Y_CHUNKS, Y_CHUNKS, rows * depth)
    size = rows * depth * width
    plane = (depth, width)
    slab = (rows, width)
    y_steps = (Y_CHUNKS - 1).bit_length()

    pair_route = [(i, i ^ 1) for i in range(nz)]
    cross_route = [(i, i + 1 if i % 2 else i - 1) for i in range(1, nz - 1)]

    def to_chip(k):
        return [(i, i ^ (2 * k)) for i in range(nz)]

    viscosity = pltpu.with_memory_space_constraint(viscosity, pltpu.HBM)
    velocity = pltpu.with_memory_space_constraint(velocity, pltpu.HBM)
    (far,) = call(
        far_kernel, [(2,) + slab], [HBM, HBM], [pltpu.SemaphoreType.DMA((2,))], 0, size
    )(viscosity, velocity)
    visc, vel, visc_z, near = call(
        load_kernel, [volume, volume, zmajor, (2,) + slab], [HBM, HBM],
        [pltpu.VMEM(zmajor, F32), pltpu.SemaphoreType.DMA((2,))], size, 6 * size,
    )(viscosity, velocity)
    pair = lax.ppermute(near, "gz", pair_route)
    cross = lax.ppermute(far, "gz", cross_route)

    half = (rows // 2, width)
    c_z, n_z, gf_z, gl_z, planes, give_c = call(
        z_factor_kernel, [zmajor] * 4 + [(3,) + half] * 2, [VMEM],
        [pltpu.VMEM(zmajor, F32)] * 2 + [pltpu.VMEM((3,) + slab, F32)], 20 * size, 5 * size,
    )(visc_z)
    c_x, n_x, gf_x, gl_x, coef, rhs0 = call(
        x_factor_kernel, [volume] * 4 + [(5,) + plane, volume], [VMEM, VMEM, HBM],
        [pltpu.VMEM(volume, F32)] * 3 + [pltpu.SemaphoreType.DMA(())], 60 * size, 9 * size,
    )(visc, vel, force)
    c_y, n_y, gf_y, gl_y, al_y, ga_y, inv_y = call(
        y_factor_kernel, [lines] * 4 + [(y_steps,) + lines[1:]] * 2 + [lines[1:]], [VMEM],
        [pltpu.VMEM(lines, F32)] * 3, 30 * size, 6 * size,
    )(visc)

    mate_c = lax.ppermute(give_c, "gz", pair_route)

    (outer_edge,) = call(outer_edge_kernel, [slab], [VMEM] * 2)(far, cross)
    w, payload = call(
        x_solve_kernel, [volume, (7,) + plane], [VMEM] * 9,
        [pltpu.VMEM(slab, F32)] * 2, 20 * size, 6 * size,
    )(visc, vel, rhs0, c_x, n_x, coef, near, pair, outer_edge)
    pair_c, chip_c = call(
        chip_factor_kernel, [(3,) + half] * 2, [VMEM] * 6, (), size, size
    )(planes, mate_c, near, far, pair, cross)
    parts = [payload] + [
        lax.ppermute(payload, "gx", [(i, i ^ k) for i in range(nx)]) for k in range(1, nx)
    ]
    dz, keep, give = call(
        make_middle_kernel(nx), [zmajor, (2,) + half, (2,) + half], [VMEM] * (nx + 13),
        [pltpu.VMEM((nx, 7) + plane, F32), pltpu.VMEM((nx + 1,) + plane, F32),
         pltpu.VMEM(lines, F32), pltpu.VMEM(lines, F32), pltpu.VMEM(zmajor, F32),
         pltpu.VMEM((2,) + slab, F32)],
        60 * size, 14 * size,
    )(*parts, w, gf_x, gl_x, vel, c_y, n_y, gf_y, gl_y, al_y, ga_y, inv_y, c_z, n_z)

    mate = lax.ppermute(give, "gz", pair_route)
    chip_ends, jump = call(pair_kernel, [(5,) + half, half], [VMEM] * 4, (), size, size)(
        keep, mate, pair_c, chip_c
    )
    others = [chip_ends] + [lax.ppermute(chip_ends, "gz", to_chip(k)) for k in range(1, chips)]
    mine, theirs = call(
        make_flux_kernel(chips), [(2,) + half] * 2, [VMEM] * (chips + 2),
        [pltpu.VMEM((chips, 5) + half, F32), pltpu.VMEM((chips + 1,) + half, F32)], size, size,
    )(*others, pair_c, jump)
    got = lax.ppermute(theirs, "gz", pair_route)
    return call(
        final_kernel, [volume], [VMEM] * 5,
        [pltpu.VMEM((4, rows // 4, depth, width), F32), pltpu.SemaphoreType.DMA((4,))],
        4 * size, 4 * size, [HBM],
    )(mine, got, dz, gf_z, gl_z)[0]


def solution(mesh):
    return jax.shard_map(
        local,
        mesh=mesh,
        in_specs=(P("gx", "gz", None), P("gx", "gz", None), P("gx", "gz", None)),
        out_specs=P("gx", "gz", None),
        check_vma=False,
    )
```

```python
import jax
import jax.numpy as jnp
from jax import lax
from jax.experimental import pallas as pl
from jax.experimental.pallas import tpu as pltpu
from jax.sharding import PartitionSpec as P

HALF_X = 0.5 * 1600.0 * 0.5
HALF_Y = 0.5 * 0.5 * 0.5
HALF_Z = 0.5 * 400.0 * 0.5
Y_CHUNKS = 8

F32 = jnp.float32
VMEM = pl.BlockSpec(memory_space=pltpu.VMEM)
HBM = pl.BlockSpec(memory_space=pltpu.HBM)


def call(kernel, outs, ins, scratch=(), flops=0, touched=0, out_specs=None):
    return pl.pallas_call(
        kernel,
        out_shape=tuple(jax.ShapeDtypeStruct(s, F32) for s in outs),
        in_specs=ins,
        out_specs=tuple(out_specs or [VMEM] * len(outs)),
        scratch_shapes=list(scratch),
        compiler_params=pltpu.CompilerParams(vmem_limit_bytes=8 << 20),
        cost_estimate=pl.CostEstimate(
            flops=flops, bytes_accessed=4 * touched, transcendentals=0
        ),
    )


def iota(shape, dim):
    return lax.broadcasted_iota(jnp.int32, shape, dim)


def shift(x, s, axis):
    return pltpu.roll(x, s % x.shape[axis], axis)


def factor(nu, rows, half, lo_term, hi_term, c_out, n_out, gf_out, gl_out, cf, cb):
    mid = rows // 2
    s, t = 1.0 + lo_term, 1.0 + hi_term
    for i in range(rows - 1):
        e = half * (nu(i) + nu(i + 1))
        r = 1.0 / (s + e)
        c = e * r
        cf[i] = c
        if i < mid:
            c_out[i] = c
            n_out[i] = r
        s = 1.0 + c * s
        if i + 1 == mid:
            s_mid = s
        j = rows - 1 - i
        e = half * (nu(j) + nu(j - 1))
        r = 1.0 / (t + e)
        c = e * r
        cb[j] = c
        if j > mid:
            c_out[j] = c
            n_out[j] = r
        t = 1.0 + c * t
        if j - 1 == mid:
            t_mid = t
    n_out[mid] = 1.0 / (s_mid + t_mid - 1.0)
    gl = 1.0 / (s + hi_term)
    gf = 1.0 / (t + lo_term)
    ends = [gf, None, gl]
    gl_out[rows - 1] = gl
    gf_out[0] = gf
    for i in range(rows - 1):
        gl = cf[rows - 2 - i] * gl
        gl_out[rows - 2 - i] = gl
        gf = cb[i + 1] * gf
        gf_out[i + 1] = gf
    ends[1] = gl
    return ends


def block_solve(rhs, rows, c, n, out):
    mid = rows // 2
    d = rhs(0)
    out[0] = d
    u = rhs(rows - 1)
    out[rows - 1] = u
    for i in range(1, mid):
        d = rhs(i) + c[i - 1] * d
        out[i] = d
        j = rows - 1 - i
        if j > mid:
            u = rhs(j) + c[j + 1] * u
            out[j] = u
    d = (rhs(mid) + c[mid - 1] * d + c[mid + 1] * u) * n[mid]
    out[mid] = d
    u = d
    for i in range(1, mid + 1):
        j = mid - i
        d = out[j] * n[j] + c[j] * d
        out[j] = d
        j = mid + i
        if j < rows:
            u = out[j] * n[j] + c[j] * u
            out[j] = u
    return d, u


def far_kernel(visc_hbm, vel_hbm, far, sems):
    rows, depth, width = visc_hbm.shape
    at = lax.rem(lax.axis_index("gz"), 2) * (depth - 1)
    copies = [
        pltpu.make_async_copy(src.at[:, at], far.at[k], sems.at[k])
        for k, src in enumerate((vel_hbm, visc_hbm))
    ]
    for copy in copies:
        copy.start()
    for copy in copies:
        copy.wait()


def load_kernel(visc_hbm, vel_hbm, visc, vel, visc_z, near, vel_z, sems):
    rows, depth, width = visc.shape
    near_at = (1 - lax.rem(lax.axis_index("gz"), 2)) * (depth - 1)
    copies = [
        pltpu.make_async_copy(src, dst, sems.at[k])
        for k, (src, dst) in enumerate(((vel_hbm, vel), (visc_hbm, visc)))
    ]
    for copy in copies:
        copy.start()
    for k, (src, turned) in enumerate(((vel, vel_z), (visc, visc_z))):
        copies[k].wait()
        turned[...] = jnp.transpose(src[...], (1, 0, 2))
        near[k] = turned[near_at]


def x_factor_kernel(visc, vel, force_hbm, c, n, gf, gl, coef, rhs, cf, cb, force, sem):
    rows, depth, width = visc.shape
    copy = pltpu.make_async_copy(force_hbm, force, sem)
    copy.start()
    lo_wall = jnp.where(lax.axis_index("gx") == 0, HALF_X, 0.0)
    hi_wall = jnp.where(lax.axis_index("gx") == lax.axis_size("gx") - 1, HALF_X, 0.0)
    ends = factor(
        lambda i: visc[i], rows, HALF_X, lo_wall * visc[0], hi_wall * visc[rows - 1],
        c, n, gf, gl, cf, cb,
    )
    for k in range(3):
        coef[k] = ends[k]
    coef[3] = visc[0]
    coef[4] = visc[rows - 1]
    block = min(rows, 16)
    lane = iota((block, depth, width), 2)
    sub = iota((block, depth, width), 1)
    copy.wait()
    for i in range(0, rows, block):
        at = slice(i, i + block)
        v = vel[at]
        nu = visc[at]
        vn = jnp.where(lane == width - 1, 0.0, shift(v, -1, 2))
        nn = jnp.where(lane == width - 1, 0.0, shift(nu, -1, 2))
        fy = (2.0 * HALF_Y) * (nu + nn) * (vn - v)
        fl = jnp.where(lane == 0, (2.0 * HALF_Y) * nu * v, shift(fy, 1, 2))
        fz = (2.0 * HALF_Z) * (nu + shift(nu, -1, 1)) * (shift(v, -1, 1) - v)
        fz = jnp.where(sub == depth - 1, 0.0, fz)
        rhs[at] = force[at] + 2.0 * v + (fy - fl) + (fz - shift(fz, 1, 1))


def split_rows(source, keep, give):
    half = keep.shape[1]
    upper = lax.rem(lax.axis_index("gz"), 2)
    keep[...] = source[:, pl.ds(pl.multiple_of(upper * half, half), half)]
    give[...] = source[:, pl.ds(pl.multiple_of((1 - upper) * half, half), half)]


def z_factor_kernel(visc_z, c, n, gf, gl, keep, give, cf, cb, planes):
    depth = visc_z.shape[0]
    lo_wall = jnp.where(lax.axis_index("gz") == 0, HALF_Z, 0.0)
    hi_wall = jnp.where(lax.axis_index("gz") == lax.axis_size("gz") - 1, HALF_Z, 0.0)
    ends = factor(
        lambda i: visc_z[i], depth, HALF_Z, lo_wall * visc_z[0], hi_wall * visc_z[depth - 1],
        c, n, gf, gl, cf, cb,
    )
    for k in range(3):
        planes[k] = ends[k]
    split_rows(planes, keep, give)


def to_lines(block):
    lines, width = block.shape
    turned = block.T.reshape(Y_CHUNKS, width // Y_CHUNKS, lines)
    return jnp.transpose(turned, (1, 0, 2))


def from_lines(block):
    length, chunks, lines = block.shape
    return jnp.transpose(block, (1, 0, 2)).reshape(length * chunks, lines).T


def y_factor_kernel(visc, c, n, gf, gl, al, ga, inv, nu, cf, cb):
    rows, depth, width = visc.shape
    length, chunks, lines = c.shape
    group = 128 // depth
    for g in range(rows // group):
        block = visc[g * group:(g + 1) * group].reshape(128, width)
        nu[:, :, g * 128:(g + 1) * 128] = to_lines(block)
    sub = iota((chunks, lines), 0)
    lo = jnp.where(sub == 0, HALF_Y * nu[0], 0.0)
    hi = jnp.where(sub == chunks - 1, HALF_Y * nu[length - 1], 0.0)
    first, across, last = factor(
        lambda i: nu[i], length, HALF_Y, lo, hi, c, n, gf, gl, cf, cb
    )
    inner = sub < chunks - 1
    e = HALF_Y * (nu[length - 1] + shift(nu[0], -1, 0))
    b = jnp.where(inner, 1.0 / e + last + shift(first, -1, 0), 1.0)
    o = jnp.where(sub < chunks - 2, shift(across, -1, 0), 0.0)
    s, k = 1, 0
    while s < chunks:
        r = 1.0 / b
        a = shift(o * r, s, 0)
        g = o * shift(r, -s, 0)
        al[k] = a
        ga[k] = g
        b = b - g * o - a * shift(o, s, 0)
        o = g * shift(o, -s, 0)
        s *= 2
        k += 1
    inv[...] = 1.0 / b


def outer_edge_kernel(far, cross, edge):
    edge[...] = (2.0 * HALF_Z) * (far[1] + cross[1]) * (cross[0] - far[0])


def x_solve_kernel(visc, vel, rhs0, c, n, coef, near, pair, by_cross_ref, w, payload, edge_lo, edge_hi):
    rows, depth, width = visc.shape
    sub = iota((depth, width), 0)
    upper = lax.rem(lax.axis_index("gz"), 2)
    two = 2.0 * HALF_Z
    by_pair = two * (near[1] + pair[1]) * (pair[0] - near[0])
    by_cross = by_cross_ref[...]
    edge_lo[...] = jnp.where(upper == 0, by_cross, by_pair)
    edge_hi[...] = jnp.where(upper == 0, by_pair, by_cross)

    def rhs(i):
        at = pl.ds(i, 1)
        lo = jnp.where(sub == 0, edge_lo[at], 0.0)
        return rhs0[i] + jnp.where(sub == depth - 1, edge_hi[at], lo)

    d, u = block_solve(rhs, rows, c, n, w)
    payload[0] = d
    payload[1] = u
    for k in range(5):
        payload[2 + k] = coef[k]


def make_middle_kernel(parts_n):
    def kernel(*refs):
        parts = refs[:parts_n]
        (w, gf, gl, vel, cy, ny, gfy, gly, aly, gay, invy, cz, nz,
         dz, keep, give, slots, flux, src, sol, turned, ends) = refs[parts_n:]
        rows, depth, width = w.shape
        me = lax.axis_index("gx")
        for k in range(parts_n):
            slots[jnp.bitwise_xor(me, k)] = parts[k][...]
        zero = jnp.zeros((depth, width), F32)
        flux[0] = zero
        flux[parts_n] = zero
        lower, source = [], []
        for f in range(parts_n - 1):
            e = HALF_X * (slots[f, 6] + slots[f + 1, 5])
            pivot = 1.0 / e + slots[f, 4] + slots[f + 1, 2]
            right = slots[f + 1, 0] - slots[f, 1]
            if f:
                pivot = pivot - slots[f, 3] * lower[-1]
                right = right + lower[-1] * source[-1]
            r = 1.0 / pivot
            lower.append(slots[f + 1, 3] * r)
            source.append(right)
            flux[f + 1] = right * r
        q = flux[parts_n - 1]
        for f in reversed(range(parts_n - 2)):
            q = flux[f + 1] + lower[f] * q
            flux[f + 1] = q
        q_left = flux[me]
        q_right = flux[me + 1]

        group = 128 // depth
        for g in range(rows // group):
            at = pl.ds(g * group, group)
            d = w[at] + q_right * gl[at] - q_left * gf[at] - 2.0 * vel[at]
            src[:, :, g * 128:(g + 1) * 128] = to_lines(d.reshape(128, width))

        length, chunks, lines = src.shape
        sub = iota((chunks, lines), 0)
        d, u = block_solve(lambda i: src[i], length, cy, ny, sol)
        q = jnp.where(sub < chunks - 1, shift(d, -1, 0) - u, 0.0)
        for k in range(aly.shape[0]):
            q = q + aly[k] * shift(q, 1 << k, 0) + gay[k] * shift(q, -(1 << k), 0)
        q = q * invy[...]
        ql = shift(q, 1, 0)
        for i in range(length):
            sol[i] = sol[i] + q * gly[i] - ql * gfy[i]
        for g in range(rows // group):
            block = from_lines(sol[:, :, g * 128:(g + 1) * 128])
            block = block.reshape(group, depth, width)
            turned[:, g * group:(g + 1) * group, :] = jnp.transpose(block, (1, 0, 2))
        d, u = block_solve(lambda i: turned[i], depth, cz, nz, dz)
        ends[0] = d
        ends[1] = u
        split_rows(ends, keep, give)

    return kernel


def chip_factor_kernel(own, mate, near, far, pair, cross, pair_c, chip_c):
    half = own.shape[1]
    upper = lax.rem(lax.axis_index("gz"), 2)
    at = pl.ds(pl.multiple_of(upper * half, half), half)
    is_low = upper == 0
    low = [jnp.where(is_low, own[k], mate[k]) for k in range(3)]
    high = [jnp.where(is_low, mate[k], own[k]) for k in range(3)]
    mid_reach = 1.0 / (HALF_Z * (near[1, at] + pair[1, at]))
    end_reach = 1.0 / (HALF_Z * (far[1, at] + cross[1, at]))
    weight = 1.0 / (mid_reach + low[2] + high[0])
    pair_c[0] = weight
    pair_c[1] = low[1]
    pair_c[2] = high[1]
    chip_c[0] = low[0] - weight * low[1] * low[1] + jnp.where(is_low, end_reach, 0.0)
    chip_c[1] = weight * low[1] * high[1]
    chip_c[2] = high[2] - weight * high[1] * high[1] + jnp.where(is_low, 0.0, end_reach)


def pair_kernel(own, mate, pair_c, payload, jump_out):
    is_low = lax.rem(lax.axis_index("gz"), 2) == 0
    low_last = jnp.where(is_low, own[1], mate[1])
    high_first = jnp.where(is_low, mate[0], own[0])
    jump = high_first - low_last
    q_mid = pair_c[0] * jump
    jump_out[...] = jump
    payload[0] = jnp.where(is_low, own[0], mate[0]) + pair_c[1] * q_mid
    payload[1] = jnp.where(is_low, mate[1], own[1]) - pair_c[2] * q_mid


def make_flux_kernel(chips):
    def kernel(*refs):
        parts, coefs = refs[:chips], refs[chips:2 * chips]
        pair_c, jump, mine, theirs, slots, flux = refs[2 * chips:]
        chip = lax.div(lax.axis_index("gz"), 2)
        is_low = lax.rem(lax.axis_index("gz"), 2) == 0
        for k in range(chips):
            at = jnp.bitwise_xor(chip, k)
            slots[at, :2] = parts[k][...]
            slots[at, 2:] = coefs[k][...]
        flux[0] = jnp.zeros_like(jump)
        flux[chips] = jnp.zeros_like(jump)
        lower, right = [], None
        for f in range(chips - 1):
            pivot = slots[f, 4] + slots[f + 1, 2]
            source = slots[f + 1, 0] - slots[f, 1]
            if f:
                pivot = pivot - slots[f, 3] * lower[-1]
                source = source + lower[-1] * right
            r = 1.0 / pivot
            lower.append(slots[f + 1, 3] * r)
            right = source
            flux[f + 1] = source * r
        q = flux[chips - 1]
        for f in reversed(range(chips - 2)):
            q = flux[f + 1] + lower[f] * q
            flux[f + 1] = q
        left, right = flux[chip], flux[chip + 1]
        mid = pair_c[0] * (jump[...] + right * pair_c[2] + left * pair_c[1])
        mine[0] = jnp.where(is_low, left, mid)
        mine[1] = jnp.where(is_low, mid, right)
        theirs[0] = jnp.where(is_low, mid, left)
        theirs[1] = jnp.where(is_low, right, mid)

    return kernel


def final_kernel(mine, got, dz, gf, gl, out, buf, sems):
    depth, rows, width = dz.shape
    parts = buf.shape[0]
    group = rows // parts
    half = rows // 2
    is_low = lax.rem(lax.axis_index("gz"), 2) == 0
    copies = []
    for p in range(parts):
        at = slice(p * group, (p + 1) * group)
        top = p * group < half
        inside = slice(p * group % half, p * group % half + group)
        own_rows = is_low if top else jnp.logical_not(is_low)
        q_left = jnp.where(own_rows, mine[0, inside], got[0, inside])
        q_right = jnp.where(own_rows, mine[1, inside], got[1, inside])
        d = dz[:, at] + q_right * gl[:, at] - q_left * gf[:, at]
        buf[p] = jnp.transpose(d, (1, 0, 2))
        copy = pltpu.make_async_copy(buf.at[p], out.at[pl.ds(p * group, group)], sems.at[p])
        copy.start()
        copies.append(copy)
    for copy in copies:
        copy.wait()


def local(velocity, viscosity, force):
    rows, depth, width = velocity.shape
    nx, nz = lax.axis_size("gx"), lax.axis_size("gz")
    chips = nz // 2
    volume = (rows, depth, width)
    zmajor = (depth, rows, width)
    lines = (width // Y_CHUNKS, Y_CHUNKS, rows * depth)
    size = rows * depth * width
    plane = (depth, width)
    slab = (rows, width)
    y_steps = (Y_CHUNKS - 1).bit_length()

    pair_route = [(i, i ^ 1) for i in range(nz)]
    cross_route = [(i, i + 1 if i % 2 else i - 1) for i in range(1, nz - 1)]

    def to_chip(k):
        return [(i, i ^ (2 * k)) for i in range(nz)]

    viscosity = pltpu.with_memory_space_constraint(viscosity, pltpu.HBM)
    velocity = pltpu.with_memory_space_constraint(velocity, pltpu.HBM)
    (far,) = call(
        far_kernel, [(2,) + slab], [HBM, HBM], [pltpu.SemaphoreType.DMA((2,))], 0, size
    )(viscosity, velocity)
    visc, vel, visc_z, near = call(
        load_kernel, [volume, volume, zmajor, (2,) + slab], [HBM, HBM],
        [pltpu.VMEM(zmajor, F32), pltpu.SemaphoreType.DMA((2,))], size, 6 * size,
    )(viscosity, velocity)
    pair = lax.ppermute(near, "gz", pair_route)
    cross = lax.ppermute(far, "gz", cross_route)

    half = (rows // 2, width)
    c_z, n_z, gf_z, gl_z, planes, give_c = call(
        z_factor_kernel, [zmajor] * 4 + [(3,) + half] * 2, [VMEM],
        [pltpu.VMEM(zmajor, F32)] * 2 + [pltpu.VMEM((3,) + slab, F32)], 20 * size, 5 * size,
    )(visc_z)
    c_x, n_x, gf_x, gl_x, coef, rhs0 = call(
        x_factor_kernel, [volume] * 4 + [(5,) + plane, volume], [VMEM, VMEM, HBM],
        [pltpu.VMEM(volume, F32)] * 3 + [pltpu.SemaphoreType.DMA(())], 60 * size, 9 * size,
    )(visc, vel, force)
    c_y, n_y, gf_y, gl_y, al_y, ga_y, inv_y = call(
        y_factor_kernel, [lines] * 4 + [(y_steps,) + lines[1:]] * 2 + [lines[1:]], [VMEM],
        [pltpu.VMEM(lines, F32)] * 3, 30 * size, 6 * size,
    )(visc)

    mate_c = lax.ppermute(give_c, "gz", pair_route)

    (outer_edge,) = call(outer_edge_kernel, [slab], [VMEM] * 2)(far, cross)
    w, payload = call(
        x_solve_kernel, [volume, (7,) + plane], [VMEM] * 9,
        [pltpu.VMEM(slab, F32)] * 2, 20 * size, 6 * size,
    )(visc, vel, rhs0, c_x, n_x, coef, near, pair, outer_edge)
    pair_c, chip_c = call(
        chip_factor_kernel, [(3,) + half] * 2, [VMEM] * 6, (), size, size
    )(planes, mate_c, near, far, pair, cross)
    parts = [payload] + [
        lax.ppermute(payload, "gx", [(i, i ^ k) for i in range(nx)]) for k in range(1, nx)
    ]
    dz, keep, give = call(
        make_middle_kernel(nx), [zmajor, (2,) + half, (2,) + half], [VMEM] * (nx + 13),
        [pltpu.VMEM((nx, 7) + plane, F32), pltpu.VMEM((nx + 1,) + plane, F32),
         pltpu.VMEM(lines, F32), pltpu.VMEM(lines, F32), pltpu.VMEM(zmajor, F32),
         pltpu.VMEM((2,) + slab, F32)],
        60 * size, 14 * size,
    )(*parts, w, gf_x, gl_x, vel, c_y, n_y, gf_y, gl_y, al_y, ga_y, inv_y, c_z, n_z)

    mate = lax.ppermute(give, "gz", pair_route)
    coefs = [chip_c] + [lax.ppermute(chip_c, "gz", to_chip(k)) for k in range(1, chips)]
    mate, *coefs = lax.optimization_barrier((mate, *coefs))
    chip_ends, jump = call(pair_kernel, [(2,) + half, half], [VMEM] * 3, (), size, size)(
        keep, mate, pair_c
    )
    others = [chip_ends] + [lax.ppermute(chip_ends, "gz", to_chip(k)) for k in range(1, chips)]
    mine, theirs = call(
        make_flux_kernel(chips), [(2,) + half] * 2, [VMEM] * (2 * chips + 2),
        [pltpu.VMEM((chips, 5) + half, F32), pltpu.VMEM((chips + 1,) + half, F32)], size, size,
    )(*others, *coefs, pair_c, jump)
    got = lax.ppermute(theirs, "gz", pair_route)
    return call(
        final_kernel, [volume], [VMEM] * 5,
        [pltpu.VMEM((4, rows // 4, depth, width), F32), pltpu.SemaphoreType.DMA((4,))],
        4 * size, 4 * size, [HBM],
    )(mine, got, dz, gf_z, gl_z)[0]


def solution(mesh):
    return jax.shard_map(
        local,
        mesh=mesh,
        in_specs=(P("gx", "gz", None), P("gx", "gz", None), P("gx", "gz", None)),
        out_specs=P("gx", "gz", None),
        check_vma=False,
    )
```

```python
import jax
import jax.numpy as jnp
from jax import lax
from jax.experimental import pallas as pl
from jax.experimental.pallas import tpu as pltpu
from jax.sharding import PartitionSpec as P

HALF_X = 0.5 * 1600.0 * 0.5
HALF_Y = 0.5 * 0.5 * 0.5
HALF_Z = 0.5 * 400.0 * 0.5
Y_CHUNKS = 8

F32 = jnp.float32
VMEM = pl.BlockSpec(memory_space=pltpu.VMEM)
HBM = pl.BlockSpec(memory_space=pltpu.HBM)


def call(kernel, outs, ins, scratch=(), flops=0, touched=0, out_specs=None):
    return pl.pallas_call(
        kernel,
        out_shape=tuple(jax.ShapeDtypeStruct(s, F32) for s in outs),
        in_specs=ins,
        out_specs=tuple(out_specs or [VMEM] * len(outs)),
        scratch_shapes=list(scratch),
        compiler_params=pltpu.CompilerParams(vmem_limit_bytes=8 << 20),
        cost_estimate=pl.CostEstimate(
            flops=flops, bytes_accessed=4 * touched, transcendentals=0
        ),
    )


def partners(n):
    return [0, *range(n - 1, 0, -1)]


def iota(shape, dim):
    return lax.broadcasted_iota(jnp.int32, shape, dim)


def shift(x, s, axis):
    return pltpu.roll(x, s % x.shape[axis], axis)


def factor(nu, rows, half, lo_term, hi_term, c_out, n_out, gf_out, gl_out, cf, cb):
    mid = rows // 2
    s, t = 1.0 + lo_term, 1.0 + hi_term
    for i in range(rows - 1):
        e = half * (nu(i) + nu(i + 1))
        r = 1.0 / (s + e)
        c = e * r
        cf[i] = c
        if i < mid:
            c_out[i] = c
            n_out[i] = r
        s = 1.0 + c * s
        if i + 1 == mid:
            s_mid = s
        j = rows - 1 - i
        e = half * (nu(j) + nu(j - 1))
        r = 1.0 / (t + e)
        c = e * r
        cb[j] = c
        if j > mid:
            c_out[j] = c
            n_out[j] = r
        t = 1.0 + c * t
        if j - 1 == mid:
            t_mid = t
    n_out[mid] = 1.0 / (s_mid + t_mid - 1.0)
    gl = 1.0 / (s + hi_term)
    gf = 1.0 / (t + lo_term)
    ends = [gf, None, gl]
    gl_out[rows - 1] = gl
    gf_out[0] = gf
    for i in range(rows - 1):
        gl = cf[rows - 2 - i] * gl
        gl_out[rows - 2 - i] = gl
        gf = cb[i + 1] * gf
        gf_out[i + 1] = gf
    ends[1] = gl
    return ends


def block_solve(rhs, rows, c, n, out):
    mid = rows // 2
    d = rhs(0)
    out[0] = d
    u = rhs(rows - 1)
    out[rows - 1] = u
    for i in range(1, mid):
        d = rhs(i) + c[i - 1] * d
        out[i] = d
        j = rows - 1 - i
        if j > mid:
            u = rhs(j) + c[j + 1] * u
            out[j] = u
    d = (rhs(mid) + c[mid - 1] * d + c[mid + 1] * u) * n[mid]
    out[mid] = d
    u = d
    for i in range(1, mid + 1):
        j = mid - i
        d = out[j] * n[j] + c[j] * d
        out[j] = d
        j = mid + i
        if j < rows:
            u = out[j] * n[j] + c[j] * u
            out[j] = u
    return d, u


def far_kernel(visc_hbm, vel_hbm, far, sems):
    rows, depth, width = visc_hbm.shape
    at = lax.rem(lax.axis_index("gz"), 2) * (depth - 1)
    copies = [
        pltpu.make_async_copy(src.at[:, at], far.at[k], sems.at[k])
        for k, src in enumerate((vel_hbm, visc_hbm))
    ]
    for copy in copies:
        copy.start()
    for copy in copies:
        copy.wait()


def load_kernel(visc_hbm, vel_hbm, visc, vel, visc_z, near, vel_z, sems):
    rows, depth, width = visc.shape
    near_at = (1 - lax.rem(lax.axis_index("gz"), 2)) * (depth - 1)
    copies = [
        pltpu.make_async_copy(src, dst, sems.at[k])
        for k, (src, dst) in enumerate(((vel_hbm, vel), (visc_hbm, visc)))
    ]
    for copy in copies:
        copy.start()
    for k, (src, turned) in enumerate(((vel, vel_z), (visc, visc_z))):
        copies[k].wait()
        turned[...] = jnp.transpose(src[...], (1, 0, 2))
        near[k] = turned[near_at]


def x_factor_kernel(visc, vel, force_hbm, c, n, gf, gl, coef, rhs, cf, cb, force, sem):
    rows, depth, width = visc.shape
    copy = pltpu.make_async_copy(force_hbm, force, sem)
    copy.start()
    lo_wall = jnp.where(lax.axis_index("gx") == 0, HALF_X, 0.0)
    hi_wall = jnp.where(lax.axis_index("gx") == lax.axis_size("gx") - 1, HALF_X, 0.0)
    ends = factor(
        lambda i: visc[i], rows, HALF_X, lo_wall * visc[0], hi_wall * visc[rows - 1],
        c, n, gf, gl, cf, cb,
    )
    for k in range(3):
        coef[k] = ends[k]
    coef[3] = visc[0]
    coef[4] = visc[rows - 1]
    block = min(rows, 16)
    lane = iota((block, depth, width), 2)
    sub = iota((block, depth, width), 1)
    copy.wait()
    for i in range(0, rows, block):
        at = slice(i, i + block)
        v = vel[at]
        nu = visc[at]
        vn = jnp.where(lane == width - 1, 0.0, shift(v, -1, 2))
        nn = jnp.where(lane == width - 1, 0.0, shift(nu, -1, 2))
        fy = (2.0 * HALF_Y) * (nu + nn) * (vn - v)
        fl = jnp.where(lane == 0, (2.0 * HALF_Y) * nu * v, shift(fy, 1, 2))
        fz = (2.0 * HALF_Z) * (nu + shift(nu, -1, 1)) * (shift(v, -1, 1) - v)
        fz = jnp.where(sub == depth - 1, 0.0, fz)
        rhs[at] = force[at] + 2.0 * v + (fy - fl) + (fz - shift(fz, 1, 1))


def split_rows(source, keep, give):
    half = keep.shape[1]
    upper = lax.rem(lax.axis_index("gz"), 2)
    keep[...] = source[:, pl.ds(pl.multiple_of(upper * half, half), half)]
    give[...] = source[:, pl.ds(pl.multiple_of((1 - upper) * half, half), half)]


def z_factor_kernel(visc_z, c, n, gf, gl, keep, give, cf, cb, planes):
    depth = visc_z.shape[0]
    lo_wall = jnp.where(lax.axis_index("gz") == 0, HALF_Z, 0.0)
    hi_wall = jnp.where(lax.axis_index("gz") == lax.axis_size("gz") - 1, HALF_Z, 0.0)
    ends = factor(
        lambda i: visc_z[i], depth, HALF_Z, lo_wall * visc_z[0], hi_wall * visc_z[depth - 1],
        c, n, gf, gl, cf, cb,
    )
    for k in range(3):
        planes[k] = ends[k]
    split_rows(planes, keep, give)


def to_lines(block):
    lines, width = block.shape
    turned = block.T.reshape(Y_CHUNKS, width // Y_CHUNKS, lines)
    return jnp.transpose(turned, (1, 0, 2))


def from_lines(block):
    length, chunks, lines = block.shape
    return jnp.transpose(block, (1, 0, 2)).reshape(length * chunks, lines).T


def y_factor_kernel(visc, c, n, gf, gl, al, ga, inv, nu, cf, cb):
    rows, depth, width = visc.shape
    length, chunks, lines = c.shape
    group = 128 // depth
    for g in range(rows // group):
        block = visc[g * group:(g + 1) * group].reshape(128, width)
        nu[:, :, g * 128:(g + 1) * 128] = to_lines(block)
    sub = iota((chunks, lines), 0)
    lo = jnp.where(sub == 0, HALF_Y * nu[0], 0.0)
    hi = jnp.where(sub == chunks - 1, HALF_Y * nu[length - 1], 0.0)
    first, across, last = factor(
        lambda i: nu[i], length, HALF_Y, lo, hi, c, n, gf, gl, cf, cb
    )
    inner = sub < chunks - 1
    e = HALF_Y * (nu[length - 1] + shift(nu[0], -1, 0))
    b = jnp.where(inner, 1.0 / e + last + shift(first, -1, 0), 1.0)
    o = jnp.where(sub < chunks - 2, shift(across, -1, 0), 0.0)
    s, k = 1, 0
    while s < chunks:
        r = 1.0 / b
        a = shift(o * r, s, 0)
        g = o * shift(r, -s, 0)
        al[k] = a
        ga[k] = g
        b = b - g * o - a * shift(o, s, 0)
        o = g * shift(o, -s, 0)
        s *= 2
        k += 1
    inv[...] = 1.0 / b


def outer_edge_kernel(far, cross, edge):
    edge[...] = (2.0 * HALF_Z) * (far[1] + cross[1]) * (cross[0] - far[0])


def x_solve_kernel(visc, vel, rhs0, c, n, coef, near, pair, by_cross_ref, w, payload, edge_lo, edge_hi):
    rows, depth, width = visc.shape
    sub = iota((depth, width), 0)
    upper = lax.rem(lax.axis_index("gz"), 2)
    two = 2.0 * HALF_Z
    by_pair = two * (near[1] + pair[1]) * (pair[0] - near[0])
    by_cross = by_cross_ref[...]
    edge_lo[...] = jnp.where(upper == 0, by_cross, by_pair)
    edge_hi[...] = jnp.where(upper == 0, by_pair, by_cross)

    def rhs(i):
        at = pl.ds(i, 1)
        lo = jnp.where(sub == 0, edge_lo[at], 0.0)
        return rhs0[i] + jnp.where(sub == depth - 1, edge_hi[at], lo)

    d, u = block_solve(rhs, rows, c, n, w)
    payload[0] = d
    payload[1] = u
    for k in range(5):
        payload[2 + k] = coef[k]


def make_middle_kernel(parts_n):
    def kernel(*refs):
        parts = refs[:parts_n]
        (w, gf, gl, vel, cy, ny, gfy, gly, aly, gay, invy, cz, nz,
         dz, keep, give, slots, flux, src, sol, turned, ends) = refs[parts_n:]
        rows, depth, width = w.shape
        me = lax.axis_index("gx")
        for k, part in zip(partners(parts_n), parts):
            slots[jnp.bitwise_xor(me, k)] = part[...]
        zero = jnp.zeros((depth, width), F32)
        flux[0] = zero
        flux[parts_n] = zero
        lower, source = [], []
        for f in range(parts_n - 1):
            e = HALF_X * (slots[f, 6] + slots[f + 1, 5])
            pivot = 1.0 / e + slots[f, 4] + slots[f + 1, 2]
            right = slots[f + 1, 0] - slots[f, 1]
            if f:
                pivot = pivot - slots[f, 3] * lower[-1]
                right = right + lower[-1] * source[-1]
            r = 1.0 / pivot
            lower.append(slots[f + 1, 3] * r)
            source.append(right)
            flux[f + 1] = right * r
        q = flux[parts_n - 1]
        for f in reversed(range(parts_n - 2)):
            q = flux[f + 1] + lower[f] * q
            flux[f + 1] = q
        q_left = flux[me]
        q_right = flux[me + 1]

        group = 128 // depth
        for g in range(rows // group):
            at = pl.ds(g * group, group)
            d = w[at] + q_right * gl[at] - q_left * gf[at] - 2.0 * vel[at]
            src[:, :, g * 128:(g + 1) * 128] = to_lines(d.reshape(128, width))

        length, chunks, lines = src.shape
        sub = iota((chunks, lines), 0)
        d, u = block_solve(lambda i: src[i], length, cy, ny, sol)
        q = jnp.where(sub < chunks - 1, shift(d, -1, 0) - u, 0.0)
        for k in range(aly.shape[0]):
            q = q + aly[k] * shift(q, 1 << k, 0) + gay[k] * shift(q, -(1 << k), 0)
        q = q * invy[...]
        ql = shift(q, 1, 0)
        for i in range(length):
            sol[i] = sol[i] + q * gly[i] - ql * gfy[i]
        for g in range(rows // group):
            block = from_lines(sol[:, :, g * 128:(g + 1) * 128])
            block = block.reshape(group, depth, width)
            turned[:, g * group:(g + 1) * group, :] = jnp.transpose(block, (1, 0, 2))
        d, u = block_solve(lambda i: turned[i], depth, cz, nz, dz)
        ends[0] = d
        ends[1] = u
        split_rows(ends, keep, give)

    return kernel


def chip_factor_kernel(own, mate, near, far, pair, cross, pair_c, chip_c):
    half = own.shape[1]
    upper = lax.rem(lax.axis_index("gz"), 2)
    at = pl.ds(pl.multiple_of(upper * half, half), half)
    is_low = upper == 0
    low = [jnp.where(is_low, own[k], mate[k]) for k in range(3)]
    high = [jnp.where(is_low, mate[k], own[k]) for k in range(3)]
    mid_reach = 1.0 / (HALF_Z * (near[1, at] + pair[1, at]))
    end_reach = 1.0 / (HALF_Z * (far[1, at] + cross[1, at]))
    weight = 1.0 / (mid_reach + low[2] + high[0])
    pair_c[0] = weight
    pair_c[1] = low[1]
    pair_c[2] = high[1]
    chip_c[0] = low[0] - weight * low[1] * low[1] + jnp.where(is_low, end_reach, 0.0)
    chip_c[1] = weight * low[1] * high[1]
    chip_c[2] = high[2] - weight * high[1] * high[1] + jnp.where(is_low, 0.0, end_reach)


def pair_kernel(own, mate, pair_c, payload, jump_out):
    is_low = lax.rem(lax.axis_index("gz"), 2) == 0
    low_last = jnp.where(is_low, own[1], mate[1])
    high_first = jnp.where(is_low, mate[0], own[0])
    jump = high_first - low_last
    q_mid = pair_c[0] * jump
    jump_out[...] = jump
    payload[0] = jnp.where(is_low, own[0], mate[0]) + pair_c[1] * q_mid
    payload[1] = jnp.where(is_low, mate[1], own[1]) - pair_c[2] * q_mid


def make_flux_kernel(chips):
    def kernel(*refs):
        parts, coefs = refs[:chips], refs[chips:2 * chips]
        pair_c, jump, mine, theirs, slots, flux = refs[2 * chips:]
        chip = lax.div(lax.axis_index("gz"), 2)
        is_low = lax.rem(lax.axis_index("gz"), 2) == 0
        for k in range(chips):
            slots[jnp.bitwise_xor(chip, k), 2:] = coefs[k][...]
        for k, part in zip(partners(chips), parts):
            slots[jnp.bitwise_xor(chip, k), :2] = part[...]
        flux[0] = jnp.zeros_like(jump)
        flux[chips] = jnp.zeros_like(jump)
        lower, right = [], None
        for f in range(chips - 1):
            pivot = slots[f, 4] + slots[f + 1, 2]
            source = slots[f + 1, 0] - slots[f, 1]
            if f:
                pivot = pivot - slots[f, 3] * lower[-1]
                source = source + lower[-1] * right
            r = 1.0 / pivot
            lower.append(slots[f + 1, 3] * r)
            right = source
            flux[f + 1] = source * r
        q = flux[chips - 1]
        for f in reversed(range(chips - 2)):
            q = flux[f + 1] + lower[f] * q
            flux[f + 1] = q
        left, right = flux[chip], flux[chip + 1]
        mid = pair_c[0] * (jump[...] + right * pair_c[2] + left * pair_c[1])
        mine[0] = jnp.where(is_low, left, mid)
        mine[1] = jnp.where(is_low, mid, right)
        theirs[0] = jnp.where(is_low, mid, left)
        theirs[1] = jnp.where(is_low, right, mid)

    return kernel


def final_kernel(mine, got, dz, gf, gl, out, buf, sems):
    depth, rows, width = dz.shape
    parts = buf.shape[0]
    group = rows // parts
    half = rows // 2
    is_low = lax.rem(lax.axis_index("gz"), 2) == 0
    copies = []
    for p in range(parts):
        at = slice(p * group, (p + 1) * group)
        top = p * group < half
        inside = slice(p * group % half, p * group % half + group)
        own_rows = is_low if top else jnp.logical_not(is_low)
        q_left = jnp.where(own_rows, mine[0, inside], got[0, inside])
        q_right = jnp.where(own_rows, mine[1, inside], got[1, inside])
        d = dz[:, at] + q_right * gl[:, at] - q_left * gf[:, at]
        buf[p] = jnp.transpose(d, (1, 0, 2))
        copy = pltpu.make_async_copy(buf.at[p], out.at[pl.ds(p * group, group)], sems.at[p])
        copy.start()
        copies.append(copy)
    for copy in copies:
        copy.wait()


def local(velocity, viscosity, force):
    rows, depth, width = velocity.shape
    nx, nz = lax.axis_size("gx"), lax.axis_size("gz")
    chips = nz // 2
    volume = (rows, depth, width)
    zmajor = (depth, rows, width)
    lines = (width // Y_CHUNKS, Y_CHUNKS, rows * depth)
    size = rows * depth * width
    plane = (depth, width)
    slab = (rows, width)
    y_steps = (Y_CHUNKS - 1).bit_length()

    pair_route = [(i, i ^ 1) for i in range(nz)]
    cross_route = [(i, i + 1 if i % 2 else i - 1) for i in range(1, nz - 1)]

    def to_chip(k):
        return [(i, i ^ (2 * k)) for i in range(nz)]

    viscosity = pltpu.with_memory_space_constraint(viscosity, pltpu.HBM)
    velocity = pltpu.with_memory_space_constraint(velocity, pltpu.HBM)
    (far,) = call(
        far_kernel, [(2,) + slab], [HBM, HBM], [pltpu.SemaphoreType.DMA((2,))], 0, size
    )(viscosity, velocity)
    visc, vel, visc_z, near = call(
        load_kernel, [volume, volume, zmajor, (2,) + slab], [HBM, HBM],
        [pltpu.VMEM(zmajor, F32), pltpu.SemaphoreType.DMA((2,))], size, 6 * size,
    )(viscosity, velocity)
    pair = lax.ppermute(near, "gz", pair_route)
    cross = lax.ppermute(far, "gz", cross_route)

    half = (rows // 2, width)
    c_z, n_z, gf_z, gl_z, planes, give_c = call(
        z_factor_kernel, [zmajor] * 4 + [(3,) + half] * 2, [VMEM],
        [pltpu.VMEM(zmajor, F32)] * 2 + [pltpu.VMEM((3,) + slab, F32)], 20 * size, 5 * size,
    )(visc_z)
    c_x, n_x, gf_x, gl_x, coef, rhs0 = call(
        x_factor_kernel, [volume] * 4 + [(5,) + plane, volume], [VMEM, VMEM, HBM],
        [pltpu.VMEM(volume, F32)] * 3 + [pltpu.SemaphoreType.DMA(())], 60 * size, 9 * size,
    )(visc, vel, force)
    c_y, n_y, gf_y, gl_y, al_y, ga_y, inv_y = call(
        y_factor_kernel, [lines] * 4 + [(y_steps,) + lines[1:]] * 2 + [lines[1:]], [VMEM],
        [pltpu.VMEM(lines, F32)] * 3, 30 * size, 6 * size,
    )(visc)

    mate_c = lax.ppermute(give_c, "gz", pair_route)

    (outer_edge,) = call(outer_edge_kernel, [slab], [VMEM] * 2)(far, cross)
    w, payload = call(
        x_solve_kernel, [volume, (7,) + plane], [VMEM] * 9,
        [pltpu.VMEM(slab, F32)] * 2, 20 * size, 6 * size,
    )(visc, vel, rhs0, c_x, n_x, coef, near, pair, outer_edge)
    pair_c, chip_c = call(
        chip_factor_kernel, [(3,) + half] * 2, [VMEM] * 6, (), size, size
    )(planes, mate_c, near, far, pair, cross)
    parts = [payload] + [
        lax.ppermute(payload, "gx", [(i, i ^ k) for i in range(nx)]) for k in range(1, nx)
    ]
    dz, keep, give = call(
        make_middle_kernel(nx), [zmajor, (2,) + half, (2,) + half], [VMEM] * (nx + 13),
        [pltpu.VMEM((nx, 7) + plane, F32), pltpu.VMEM((nx + 1,) + plane, F32),
         pltpu.VMEM(lines, F32), pltpu.VMEM(lines, F32), pltpu.VMEM(zmajor, F32),
         pltpu.VMEM((2,) + slab, F32)],
        60 * size, 14 * size,
    )(*[parts[k] for k in partners(nx)], w, gf_x, gl_x, vel, c_y, n_y, gf_y, gl_y, al_y, ga_y, inv_y, c_z, n_z)

    mate = lax.ppermute(give, "gz", pair_route)
    coefs = [chip_c] + [lax.ppermute(chip_c, "gz", to_chip(k)) for k in range(1, chips)]
    mate, *coefs = lax.optimization_barrier((mate, *coefs))
    chip_ends, jump = call(pair_kernel, [(2,) + half, half], [VMEM] * 3, (), size, size)(
        keep, mate, pair_c
    )
    others = [chip_ends] + [lax.ppermute(chip_ends, "gz", to_chip(k)) for k in range(1, chips)]
    mine, theirs = call(
        make_flux_kernel(chips), [(2,) + half] * 2, [VMEM] * (2 * chips + 2),
        [pltpu.VMEM((chips, 5) + half, F32), pltpu.VMEM((chips + 1,) + half, F32)], size, size,
    )(*[others[k] for k in partners(chips)], *coefs, pair_c, jump)
    got = lax.ppermute(theirs, "gz", pair_route)
    return call(
        final_kernel, [volume], [VMEM] * 5,
        [pltpu.VMEM((4, rows // 4, depth, width), F32), pltpu.SemaphoreType.DMA((4,))],
        4 * size, 4 * size, [HBM],
    )(mine, got, dz, gf_z, gl_z)[0]


def solution(mesh):
    return jax.shard_map(
        local,
        mesh=mesh,
        in_specs=(P("gx", "gz", None), P("gx", "gz", None), P("gx", "gz", None)),
        out_specs=P("gx", "gz", None),
        check_vma=False,
    )
```

```python
import jax
import jax.numpy as jnp
from jax import lax
from jax.experimental import pallas as pl
from jax.experimental.pallas import tpu as pltpu
from jax.sharding import PartitionSpec as P

HALF_X = 0.5 * 1600.0 * 0.5
HALF_Y = 0.5 * 0.5 * 0.5
HALF_Z = 0.5 * 400.0 * 0.5
Y_CHUNKS = 8

F32 = jnp.float32
VMEM = pl.BlockSpec(memory_space=pltpu.VMEM)
HBM = pl.BlockSpec(memory_space=pltpu.HBM)


def call(kernel, outs, ins, scratch=(), flops=0, touched=0, out_specs=None):
    return pl.pallas_call(
        kernel,
        out_shape=tuple(jax.ShapeDtypeStruct(s, F32) for s in outs),
        in_specs=ins,
        out_specs=tuple(out_specs or [VMEM] * len(outs)),
        scratch_shapes=list(scratch),
        compiler_params=pltpu.CompilerParams(vmem_limit_bytes=8 << 20),
        cost_estimate=pl.CostEstimate(
            flops=flops, bytes_accessed=4 * touched, transcendentals=0
        ),
    )


def partners(n):
    return [0, *range(n - 1, 0, -1)]


def iota(shape, dim):
    return lax.broadcasted_iota(jnp.int32, shape, dim)


def shift(x, s, axis):
    return pltpu.roll(x, s % x.shape[axis], axis)


def factor(nu, rows, half, lo_term, hi_term, c_out, n_out, gf_out, gl_out, cf, cb):
    mid = rows // 2
    s, t = 1.0 + lo_term, 1.0 + hi_term
    for i in range(rows - 1):
        e = half * (nu(i) + nu(i + 1))
        r = 1.0 / (s + e)
        c = e * r
        cf[i] = c
        if i < mid:
            c_out[i] = c
            n_out[i] = r
        s = 1.0 + c * s
        if i + 1 == mid:
            s_mid = s
        j = rows - 1 - i
        e = half * (nu(j) + nu(j - 1))
        r = 1.0 / (t + e)
        c = e * r
        cb[j] = c
        if j > mid:
            c_out[j] = c
            n_out[j] = r
        t = 1.0 + c * t
        if j - 1 == mid:
            t_mid = t
    n_out[mid] = 1.0 / (s_mid + t_mid - 1.0)
    gl = 1.0 / (s + hi_term)
    gf = 1.0 / (t + lo_term)
    ends = [gf, None, gl]
    gl_out[rows - 1] = gl
    gf_out[0] = gf
    for i in range(rows - 1):
        gl = cf[rows - 2 - i] * gl
        gl_out[rows - 2 - i] = gl
        gf = cb[i + 1] * gf
        gf_out[i + 1] = gf
    ends[1] = gl
    return ends


def block_solve(rhs, rows, c, n, out):
    mid = rows // 2
    d = rhs(0)
    out[0] = d
    u = rhs(rows - 1)
    out[rows - 1] = u
    for i in range(1, mid):
        d = rhs(i) + c[i - 1] * d
        out[i] = d
        j = rows - 1 - i
        if j > mid:
            u = rhs(j) + c[j + 1] * u
            out[j] = u
    d = (rhs(mid) + c[mid - 1] * d + c[mid + 1] * u) * n[mid]
    out[mid] = d
    u = d
    for i in range(1, mid + 1):
        j = mid - i
        d = out[j] * n[j] + c[j] * d
        out[j] = d
        j = mid + i
        if j < rows:
            u = out[j] * n[j] + c[j] * u
            out[j] = u
    return d, u


def far_kernel(visc_hbm, vel_hbm, far, sems):
    rows, depth, width = visc_hbm.shape
    at = lax.rem(lax.axis_index("gz"), 2) * (depth - 1)
    copies = [
        pltpu.make_async_copy(src.at[:, at], far.at[k], sems.at[k])
        for k, src in enumerate((vel_hbm, visc_hbm))
    ]
    for copy in copies:
        copy.start()
    for copy in copies:
        copy.wait()


def load_kernel(visc_hbm, vel_hbm, visc, vel, visc_z, near, vel_z, sems):
    rows, depth, width = visc.shape
    near_at = (1 - lax.rem(lax.axis_index("gz"), 2)) * (depth - 1)
    copies = [
        pltpu.make_async_copy(src, dst, sems.at[k])
        for k, (src, dst) in enumerate(((vel_hbm, vel), (visc_hbm, visc)))
    ]
    for copy in copies:
        copy.start()
    for k, (src, turned) in enumerate(((vel, vel_z), (visc, visc_z))):
        copies[k].wait()
        turned[...] = jnp.transpose(src[...], (1, 0, 2))
        near[k] = turned[near_at]


def x_factor_kernel(visc, vel, force_hbm, c, n, gf, gl, coef, rhs, cf, cb, force, sem):
    rows, depth, width = visc.shape
    copy = pltpu.make_async_copy(force_hbm, force, sem)
    copy.start()
    lo_wall = jnp.where(lax.axis_index("gx") == 0, HALF_X, 0.0)
    hi_wall = jnp.where(lax.axis_index("gx") == lax.axis_size("gx") - 1, HALF_X, 0.0)
    ends = factor(
        lambda i: visc[i], rows, HALF_X, lo_wall * visc[0], hi_wall * visc[rows - 1],
        c, n, gf, gl, cf, cb,
    )
    for k in range(3):
        coef[k] = ends[k]
    coef[3] = visc[0]
    coef[4] = visc[rows - 1]
    block = min(rows, 16)
    lane = iota((block, depth, width), 2)
    sub = iota((block, depth, width), 1)
    copy.wait()
    for i in range(0, rows, block):
        at = slice(i, i + block)
        v = vel[at]
        nu = visc[at]
        vn = jnp.where(lane == width - 1, 0.0, shift(v, -1, 2))
        nn = jnp.where(lane == width - 1, 0.0, shift(nu, -1, 2))
        fy = (2.0 * HALF_Y) * (nu + nn) * (vn - v)
        fl = jnp.where(lane == 0, (2.0 * HALF_Y) * nu * v, shift(fy, 1, 2))
        fz = (2.0 * HALF_Z) * (nu + shift(nu, -1, 1)) * (shift(v, -1, 1) - v)
        fz = jnp.where(sub == depth - 1, 0.0, fz)
        rhs[at] = force[at] + 2.0 * v + (fy - fl) + (fz - shift(fz, 1, 1))


def split_rows(source, keep, give):
    half = keep.shape[1]
    upper = lax.rem(lax.axis_index("gz"), 2)
    keep[...] = source[:, pl.ds(pl.multiple_of(upper * half, half), half)]
    give[...] = source[:, pl.ds(pl.multiple_of((1 - upper) * half, half), half)]


def z_factor_kernel(visc_z, c, n, gf, gl, keep, give, cf, cb, planes):
    depth = visc_z.shape[0]
    lo_wall = jnp.where(lax.axis_index("gz") == 0, HALF_Z, 0.0)
    hi_wall = jnp.where(lax.axis_index("gz") == lax.axis_size("gz") - 1, HALF_Z, 0.0)
    ends = factor(
        lambda i: visc_z[i], depth, HALF_Z, lo_wall * visc_z[0], hi_wall * visc_z[depth - 1],
        c, n, gf, gl, cf, cb,
    )
    for k in range(3):
        planes[k] = ends[k]
    split_rows(planes, keep, give)


def to_lines(block):
    lines, width = block.shape
    turned = block.T.reshape(Y_CHUNKS, width // Y_CHUNKS, lines)
    return jnp.transpose(turned, (1, 0, 2))


def from_lines(block):
    length, chunks, lines = block.shape
    return jnp.transpose(block, (1, 0, 2)).reshape(length * chunks, lines).T


def y_factor_kernel(visc, c, n, gf, gl, al, ga, inv, nu, cf, cb):
    rows, depth, width = visc.shape
    length, chunks, lines = c.shape
    group = 128 // depth
    for g in range(rows // group):
        block = visc[g * group:(g + 1) * group].reshape(128, width)
        nu[:, :, g * 128:(g + 1) * 128] = to_lines(block)
    sub = iota((chunks, lines), 0)
    lo = jnp.where(sub == 0, HALF_Y * nu[0], 0.0)
    hi = jnp.where(sub == chunks - 1, HALF_Y * nu[length - 1], 0.0)
    first, across, last = factor(
        lambda i: nu[i], length, HALF_Y, lo, hi, c, n, gf, gl, cf, cb
    )
    inner = sub < chunks - 1
    e = HALF_Y * (nu[length - 1] + shift(nu[0], -1, 0))
    b = jnp.where(inner, 1.0 / e + last + shift(first, -1, 0), 1.0)
    o = jnp.where(sub < chunks - 2, shift(across, -1, 0), 0.0)
    s, k = 1, 0
    while s < chunks:
        r = 1.0 / b
        a = shift(o * r, s, 0)
        g = o * shift(r, -s, 0)
        al[k] = a
        ga[k] = g
        b = b - g * o - a * shift(o, s, 0)
        o = g * shift(o, -s, 0)
        s *= 2
        k += 1
    inv[...] = 1.0 / b


def outer_edge_kernel(far, cross, edge):
    edge[...] = (2.0 * HALF_Z) * (far[1] + cross[1]) * (cross[0] - far[0])


def x_solve_kernel(visc, vel, rhs0, c, n, coef, near, pair, by_cross_ref, w, payload, edge_lo, edge_hi):
    rows, depth, width = visc.shape
    sub = iota((depth, width), 0)
    upper = lax.rem(lax.axis_index("gz"), 2)
    two = 2.0 * HALF_Z
    by_pair = two * (near[1] + pair[1]) * (pair[0] - near[0])
    by_cross = by_cross_ref[...]
    edge_lo[...] = jnp.where(upper == 0, by_cross, by_pair)
    edge_hi[...] = jnp.where(upper == 0, by_pair, by_cross)

    def rhs(i):
        at = pl.ds(i, 1)
        lo = jnp.where(sub == 0, edge_lo[at], 0.0)
        return rhs0[i] + jnp.where(sub == depth - 1, edge_hi[at], lo)

    d, u = block_solve(rhs, rows, c, n, w)
    payload[0] = d
    payload[1] = u
    for k in range(5):
        payload[2 + k] = coef[k]


def make_middle_kernel(parts_n):
    def kernel(*refs):
        parts = refs[:parts_n]
        (w, gf, gl, vel, cy, ny, gfy, gly, aly, gay, invy, cz, nz,
         dz, keep, give, slots, flux, src, sol, turned, ends) = refs[parts_n:]
        rows, depth, width = w.shape
        me = lax.axis_index("gx")
        for k, part in zip(partners(parts_n), parts):
            slots[jnp.bitwise_xor(me, k)] = part[...]
        zero = jnp.zeros((depth, width), F32)
        flux[0] = zero
        flux[parts_n] = zero
        lower, source = [], []
        for f in range(parts_n - 1):
            e = HALF_X * (slots[f, 6] + slots[f + 1, 5])
            pivot = 1.0 / e + slots[f, 4] + slots[f + 1, 2]
            right = slots[f + 1, 0] - slots[f, 1]
            if f:
                pivot = pivot - slots[f, 3] * lower[-1]
                right = right + lower[-1] * source[-1]
            r = 1.0 / pivot
            lower.append(slots[f + 1, 3] * r)
            source.append(right)
            flux[f + 1] = right * r
        q = flux[parts_n - 1]
        for f in reversed(range(parts_n - 2)):
            q = flux[f + 1] + lower[f] * q
            flux[f + 1] = q
        q_left = flux[me]
        q_right = flux[me + 1]

        group = 128 // depth
        for g in range(rows // group):
            at = pl.ds(g * group, group)
            d = w[at] + q_right * gl[at] - q_left * gf[at] - 2.0 * vel[at]
            src[:, :, g * 128:(g + 1) * 128] = to_lines(d.reshape(128, width))

        length, chunks, lines = src.shape
        sub = iota((chunks, lines), 0)
        d, u = block_solve(lambda i: src[i], length, cy, ny, sol)
        q = jnp.where(sub < chunks - 1, shift(d, -1, 0) - u, 0.0)
        for k in range(aly.shape[0]):
            q = q + aly[k] * shift(q, 1 << k, 0) + gay[k] * shift(q, -(1 << k), 0)
        q = q * invy[...]
        ql = shift(q, 1, 0)
        for i in range(length):
            sol[i] = sol[i] + q * gly[i] - ql * gfy[i]
        for g in range(rows // group):
            block = from_lines(sol[:, :, g * 128:(g + 1) * 128])
            block = block.reshape(group, depth, width)
            turned[:, g * group:(g + 1) * group, :] = jnp.transpose(block, (1, 0, 2))
        d, u = block_solve(lambda i: turned[i], depth, cz, nz, dz)
        ends[0] = d
        ends[1] = u
        split_rows(ends, keep, give)

    return kernel


def chip_factor_kernel(own, mate, near, far, pair, cross, pair_c, chip_c):
    half = own.shape[1]
    upper = lax.rem(lax.axis_index("gz"), 2)
    at = pl.ds(pl.multiple_of(upper * half, half), half)
    is_low = upper == 0
    low = [jnp.where(is_low, own[k], mate[k]) for k in range(3)]
    high = [jnp.where(is_low, mate[k], own[k]) for k in range(3)]
    mid_reach = 1.0 / (HALF_Z * (near[1, at] + pair[1, at]))
    end_reach = 1.0 / (HALF_Z * (far[1, at] + cross[1, at]))
    weight = 1.0 / (mid_reach + low[2] + high[0])
    pair_c[0] = weight
    pair_c[1] = low[1]
    pair_c[2] = high[1]
    chip_c[0] = low[0] - weight * low[1] * low[1] + jnp.where(is_low, end_reach, 0.0)
    chip_c[1] = weight * low[1] * high[1]
    chip_c[2] = high[2] - weight * high[1] * high[1] + jnp.where(is_low, 0.0, end_reach)


def pair_kernel(own, mate, pair_c, payload, jump_out):
    is_low = lax.rem(lax.axis_index("gz"), 2) == 0
    low_last = jnp.where(is_low, own[1], mate[1])
    high_first = jnp.where(is_low, mate[0], own[0])
    jump = high_first - low_last
    q_mid = pair_c[0] * jump
    jump_out[...] = jump
    payload[0] = jnp.where(is_low, own[0], mate[0]) + pair_c[1] * q_mid
    payload[1] = jnp.where(is_low, mate[1], own[1]) - pair_c[2] * q_mid


def make_flux_kernel(chips):
    def kernel(*refs):
        parts, coefs = refs[:chips], refs[chips:2 * chips]
        pair_c, jump, mine, theirs, slots, flux = refs[2 * chips:]
        chip = lax.div(lax.axis_index("gz"), 2)
        is_low = lax.rem(lax.axis_index("gz"), 2) == 0
        for k, part, coef in zip(partners(chips), parts, coefs):
            slots[jnp.bitwise_xor(chip, k), :2] = part[...]
            slots[jnp.bitwise_xor(chip, k), 2:] = coef[...]
        flux[0] = jnp.zeros_like(jump)
        flux[chips] = jnp.zeros_like(jump)
        lower, right = [], None
        for f in range(chips - 1):
            pivot = slots[f, 4] + slots[f + 1, 2]
            source = slots[f + 1, 0] - slots[f, 1]
            if f:
                pivot = pivot - slots[f, 3] * lower[-1]
                source = source + lower[-1] * right
            r = 1.0 / pivot
            lower.append(slots[f + 1, 3] * r)
            right = source
            flux[f + 1] = source * r
        q = flux[chips - 1]
        for f in reversed(range(chips - 2)):
            q = flux[f + 1] + lower[f] * q
            flux[f + 1] = q
        left, right = flux[chip], flux[chip + 1]
        mid = pair_c[0] * (jump[...] + right * pair_c[2] + left * pair_c[1])
        mine[0] = jnp.where(is_low, left, mid)
        mine[1] = jnp.where(is_low, mid, right)
        theirs[0] = jnp.where(is_low, mid, left)
        theirs[1] = jnp.where(is_low, right, mid)

    return kernel


def final_kernel(mine, got, dz, gf, gl, out, buf, sems):
    depth, rows, width = dz.shape
    parts = buf.shape[0]
    group = rows // parts
    half = rows // 2
    is_low = lax.rem(lax.axis_index("gz"), 2) == 0
    copies = []
    for p in range(parts):
        at = slice(p * group, (p + 1) * group)
        top = p * group < half
        inside = slice(p * group % half, p * group % half + group)
        own_rows = is_low if top else jnp.logical_not(is_low)
        q_left = jnp.where(own_rows, mine[0, inside], got[0, inside])
        q_right = jnp.where(own_rows, mine[1, inside], got[1, inside])
        d = dz[:, at] + q_right * gl[:, at] - q_left * gf[:, at]
        buf[p] = jnp.transpose(d, (1, 0, 2))
        copy = pltpu.make_async_copy(buf.at[p], out.at[pl.ds(p * group, group)], sems.at[p])
        copy.start()
        copies.append(copy)
    for copy in copies:
        copy.wait()


def local(velocity, viscosity, force):
    rows, depth, width = velocity.shape
    nx, nz = lax.axis_size("gx"), lax.axis_size("gz")
    chips = nz // 2
    volume = (rows, depth, width)
    zmajor = (depth, rows, width)
    lines = (width // Y_CHUNKS, Y_CHUNKS, rows * depth)
    size = rows * depth * width
    plane = (depth, width)
    slab = (rows, width)
    y_steps = (Y_CHUNKS - 1).bit_length()

    pair_route = [(i, i ^ 1) for i in range(nz)]
    cross_route = [(i, i + 1 if i % 2 else i - 1) for i in range(1, nz - 1)]

    def to_chip(k):
        return [(i, i ^ (2 * k)) for i in range(nz)]

    viscosity = pltpu.with_memory_space_constraint(viscosity, pltpu.HBM)
    velocity = pltpu.with_memory_space_constraint(velocity, pltpu.HBM)
    (far,) = call(
        far_kernel, [(2,) + slab], [HBM, HBM], [pltpu.SemaphoreType.DMA((2,))], 0, size
    )(viscosity, velocity)
    visc, vel, visc_z, near = call(
        load_kernel, [volume, volume, zmajor, (2,) + slab], [HBM, HBM],
        [pltpu.VMEM(zmajor, F32), pltpu.SemaphoreType.DMA((2,))], size, 6 * size,
    )(viscosity, velocity)
    pair = lax.ppermute(near, "gz", pair_route)
    cross = lax.ppermute(far, "gz", cross_route)

    half = (rows // 2, width)
    c_z, n_z, gf_z, gl_z, planes, give_c = call(
        z_factor_kernel, [zmajor] * 4 + [(3,) + half] * 2, [VMEM],
        [pltpu.VMEM(zmajor, F32)] * 2 + [pltpu.VMEM((3,) + slab, F32)], 20 * size, 5 * size,
    )(visc_z)
    c_x, n_x, gf_x, gl_x, coef, rhs0 = call(
        x_factor_kernel, [volume] * 4 + [(5,) + plane, volume], [VMEM, VMEM, HBM],
        [pltpu.VMEM(volume, F32)] * 3 + [pltpu.SemaphoreType.DMA(())], 60 * size, 9 * size,
    )(visc, vel, force)
    c_y, n_y, gf_y, gl_y, al_y, ga_y, inv_y = call(
        y_factor_kernel, [lines] * 4 + [(y_steps,) + lines[1:]] * 2 + [lines[1:]], [VMEM],
        [pltpu.VMEM(lines, F32)] * 3, 30 * size, 6 * size,
    )(visc)

    mate_c = lax.ppermute(give_c, "gz", pair_route)

    (outer_edge,) = call(outer_edge_kernel, [slab], [VMEM] * 2)(far, cross)
    w, payload = call(
        x_solve_kernel, [volume, (7,) + plane], [VMEM] * 9,
        [pltpu.VMEM(slab, F32)] * 2, 20 * size, 6 * size,
    )(visc, vel, rhs0, c_x, n_x, coef, near, pair, outer_edge)
    pair_c, chip_c = call(
        chip_factor_kernel, [(3,) + half] * 2, [VMEM] * 6, (), size, size
    )(planes, mate_c, near, far, pair, cross)
    parts = [payload] + [
        lax.ppermute(payload, "gx", [(i, i ^ k) for i in range(nx)]) for k in range(1, nx)
    ]
    dz, keep, give = call(
        make_middle_kernel(nx), [zmajor, (2,) + half, (2,) + half], [VMEM] * (nx + 13),
        [pltpu.VMEM((nx, 7) + plane, F32), pltpu.VMEM((nx + 1,) + plane, F32),
         pltpu.VMEM(lines, F32), pltpu.VMEM(lines, F32), pltpu.VMEM(zmajor, F32),
         pltpu.VMEM((2,) + slab, F32)],
        60 * size, 14 * size,
    )(*[parts[k] for k in partners(nx)], w, gf_x, gl_x, vel, c_y, n_y, gf_y, gl_y, al_y, ga_y, inv_y, c_z, n_z)

    mate = lax.ppermute(give, "gz", pair_route)
    coefs = [chip_c] + [lax.ppermute(chip_c, "gz", to_chip(k)) for k in partners(chips)[1:]]
    mate, *coefs = lax.optimization_barrier((mate, *coefs))
    chip_ends, jump = call(pair_kernel, [(2,) + half, half], [VMEM] * 3, (), size, size)(
        keep, mate, pair_c
    )
    others = [chip_ends] + [lax.ppermute(chip_ends, "gz", to_chip(k)) for k in range(1, chips)]
    mine, theirs = call(
        make_flux_kernel(chips), [(2,) + half] * 2, [VMEM] * (2 * chips + 2),
        [pltpu.VMEM((chips, 5) + half, F32), pltpu.VMEM((chips + 1,) + half, F32)], size, size,
    )(*[others[k] for k in partners(chips)], *coefs, pair_c, jump)
    got = lax.ppermute(theirs, "gz", pair_route)
    return call(
        final_kernel, [volume], [VMEM] * 5,
        [pltpu.VMEM((4, rows // 4, depth, width), F32), pltpu.SemaphoreType.DMA((4,))],
        4 * size, 4 * size, [HBM],
    )(mine, got, dz, gf_z, gl_z)[0]


def solution(mesh):
    return jax.shard_map(
        local,
        mesh=mesh,
        in_specs=(P("gx", "gz", None), P("gx", "gz", None), P("gx", "gz", None)),
        out_specs=P("gx", "gz", None),
        check_vma=False,
    )
```
